256 devices in a mesh: cuts: 16 (over z, core), rank: 16 (over x, y).
Axes of the slice: x: 4, y: 4, z: 8, core: 2. Of those that a mesh axis runs over, the one named last changes fastest.
Arguments:
- core_one: float32 [512, 320, 512], P('rank', 'cuts'), may hold values from -6 to 6
- core_two: float32 [512, 320, 512], P('rank', 'cuts'), may hold values from -0.25 to 0.25
- right_sketch: float32 [512, 128], replicated, may hold values from -0.25 to 0.25
- sketch_core: float32 [128, 320, 128], P(None, 'cuts'), may hold values from -0.03125 to 0.03125
Outputs:
- left_core: float32 [512, 320, 128], P('rank', 'cuts')
- middle_core: float32 [128, 320, 128], P('rank', 'cuts')
- carry: float32 [128, 512], replicated
The draws below stay inside these ranges and needn't reach their ends.
All inputs are finite; a program needn't handle non-finite values.
Results may differ from the reference program's by a relative error of at most 0.00015.
Values sent between devices are 32-bit elements; how exact they have to be, the bound alone decides.
A program may use at most 64 MiB of HBM per device.

```python
import jax
import jax.numpy as jnp
from jax import lax

R = 512
NM = 320
L = 128


def shard_levels(own_key, extent, pieces, low, top_value):
    level, own = 1.0, jax.random.fold_in(own_key, 6)
    for position, shards_of in pieces:
        draws = jnp.exp(jax.random.uniform(jax.random.fold_in(own, position), (shards_of,), jnp.float32, low / len(pieces), top_value / len(pieces)))
        level = level * jnp.repeat(draws, extent[position] // shards_of).reshape([-1 if axis == position else 1 for axis in range(len(extent))])
    return level


def normal_values(key, extent, width, reach, pieces=(), held_as=jnp.bfloat16):
    result = width * jax.random.normal(key, extent, jnp.float32)
    if pieces:
        result = result * shard_levels(key, extent, pieces, -0.22, 0.18)
    return jnp.clip(result, -reach, reach).astype(held_as)


def setup_inputs(seed: int = 0) -> dict:
    arg_keys = jax.random.split(jax.random.key(seed), 5)
    return {
        "core_one": normal_values(arg_keys[0], (R, NM, R), 1.0, 6.0, ((0, 16), (1, 16)), jnp.float32),
        "core_two": normal_values(arg_keys[1], (R, NM, R), R ** -0.5, 0.25, ((0, 16), (1, 16)), jnp.float32),
        "right_sketch": normal_values(arg_keys[2], (R, L), R ** -0.5, 0.25, (), jnp.float32),
        "sketch_core": normal_values(arg_keys[3], (L, NM, L), (NM * L) ** -0.5, 0.03125, ((1, 16),), jnp.float32),
    }


def orthonormalize(rows, unfolded):
    highest = lax.Precision.HIGHEST
    gram = jnp.dot(rows.T.astype(jnp.float32), rows.astype(jnp.float32), precision=highest, preferred_element_type=jnp.float32)
    factor = jnp.linalg.cholesky(gram)
    ortho = lax.linalg.triangular_solve(factor, rows, left_side=False, lower=True, transpose_a=True)
    carried = jnp.dot(ortho.T.astype(jnp.float32), unfolded.astype(jnp.float32), precision=highest, preferred_element_type=jnp.float32)
    return (ortho, carried)

def reference(core_one, core_two, right_sketch, sketch_core):
    highest = lax.Precision.HIGHEST
    sketched = jnp.einsum('anj,jc->anc', core_two, right_sketch, precision=highest)
    bridge = jnp.einsum('anc,bnc->ab', sketched, sketch_core, precision=highest)
    flat_one = core_one.reshape(R * NM, R)
    first_rows = jnp.dot(flat_one.astype(jnp.float32), bridge.astype(jnp.float32), precision=highest, preferred_element_type=jnp.float32)
    first_q, first_carry = orthonormalize(first_rows, flat_one)
    projected = jnp.einsum('ba,ank->bnk', first_carry, core_two, precision=highest)
    flat_two = projected.reshape(L * NM, R)
    second_rows = jnp.dot(flat_two.astype(jnp.float32), right_sketch.astype(jnp.float32), precision=highest, preferred_element_type=jnp.float32)
    second_q, carry = orthonormalize(second_rows, flat_two)
    left_core = (jnp.sqrt(jnp.float32(R * NM)) * first_q).reshape(R, NM, L)
    middle_core = (jnp.sqrt(jnp.float32(L * NM)) * second_q).reshape(L, NM, L)
    return (left_core, middle_core, carry)
```

```python
import functools
import math

import jax
import jax.numpy as jnp
from jax import lax
from jax.experimental import pallas as pl
from jax.experimental.pallas import tpu as pltpu
from jax.sharding import PartitionSpec as P

MESH = pl.DeviceIdType.MESH
F32 = jnp.float32
BF16 = jnp.bfloat16
NN = (((1,), (0,)), ((), ()))
NT = (((1,), (1,)), ((), ()))
TN = (((0,), (0,)), ((), ()))


def split(value):
    high = value.astype(BF16)
    return high, (value - high.astype(F32)).astype(BF16)


def product(left, right, dims):
    (left_high, left_low), (right_high, right_low) = left, right
    dot = functools.partial(lax.dot_general, dimension_numbers=dims, preferred_element_type=F32)
    return dot(left_high, right_high) + (dot(left_high, right_low) + dot(left_low, right_high))


def exact(left, right, dims):
    return lax.dot_general(
        left, right, dims, precision=lax.Precision.HIGHEST, preferred_element_type=F32
    )


def inverse_factor(gram_ref, width):
    blocks = width // 8
    lane = lax.broadcasted_iota(jnp.int32, (8, width), 1)
    row = lax.broadcasted_iota(jnp.int32, (8, width), 0)
    unit = (lane == row).astype(F32)
    block_of = lax.broadcasted_iota(jnp.int32, (blocks, 8, width), 0)
    first_lanes = lax.broadcasted_iota(jnp.int32, (blocks, 8, width), 2) < 8

    def spread(value, i):
        return jnp.broadcast_to(value[i : i + 1, :], (8, width))

    def step(block, carry):
        start = pl.multiple_of(block * 8, 8)
        own = gram_ref[pl.ds(start, 8), :]
        column = [jnp.broadcast_to(own[:, m : m + 1], (8, width)) for m in range(8)]
        entry = [[spread(column[m], i) if m <= i else None for m in range(8)] for i in range(8)]
        replaced = jnp.where(lane < 8, unit, own)
        rows = [spread(replaced, i) for i in range(8)]
        inverse, solved = [], []
        for j in range(8):
            inverse.append(lax.rsqrt(entry[j][j]))
            solved.append(rows[j] * inverse[j])
            for i in range(j + 1, 8):
                entry[i][j] = entry[i][j] * inverse[j]
            for i in range(j + 1, 8):
                rows[i] = rows[i] - entry[i][j] * solved[j]
                for m in range(j + 1, i + 1):
                    entry[i][m] = entry[i][m] - entry[i][j] * entry[m][j]
        back = list(solved)
        for j in reversed(range(8)):
            for i in range(j + 1, 8):
                back[j] = back[j] - entry[i][j] * back[i]
            back[j] = back[j] * inverse[j]
        done = solved[0]
        for j in range(1, 8):
            done = jnp.where(row == j, solved[j], done)
        whole = gram_ref[...].reshape(blocks, 8, width)
        update = jnp.where(first_lanes, 0.0, whole)
        for m in range(8):
            update = update - whole[:, :, m : m + 1] * back[m][None]
        whole = jnp.where(block_of > block, update, jnp.where(block_of == block, done[None], whole))
        gram_ref[...] = pltpu.roll(whole.reshape(width, width), width - 8, 1)
        return carry

    lax.fori_loop(0, blocks, step, 0)
    lower = lax.broadcasted_iota(jnp.int32, (width, width), 0) >= lax.broadcasted_iota(
        jnp.int32, (width, width), 1
    )
    gram_ref[...] = jnp.where(lower, gram_ref[...], 0.0)


def kernel(
    n_cuts, n_rank, scale_left, scale_middle,
    one_ref, two_ref, sketch_ref, core_ref, left_ref, middle_ref, carry_ref,
    one_high, one_low, bridge_part, bridge_recv, bridge,
    first_rows, full_two, projected, second_rows, returned, gram,
    reduce_part, reduce_recv, reduce_sum, gather_recv, gather_sum, reduced,
    send_sem, recv_sem, two_send, two_recv, back_send, back_recv,
):
    slices, local, width = one_ref.shape
    out_width = sketch_ref.shape[1]
    band = out_width // n_rank
    chunk = out_width // n_cuts
    my_cut, my_rank = lax.axis_index("cuts"), lax.axis_index("rank")
    full, extra = slices // n_rank, slices % n_rank
    stride = max((n_rank - 1) // (extra - 1), 1) if extra > 1 else 1
    slots = full + (1 if extra else 0)

    def owner(n):
        return n % n_rank if n < full * n_rank else (n - full * n_rank) * stride

    def has_extra(rank):
        return jnp.logical_and(lax.rem(rank, stride) == 0, lax.div(rank, stride) < extra)

    def cut_device(k):
        peer = lax.rem(my_cut + k, n_cuts)
        return peer, (peer, my_rank)

    def rank_device(k):
        peer = lax.rem(my_rank + k, n_rank)
        return peer, (my_cut, peer)

    def remote(source, target, send, recv, device):
        return pltpu.make_async_remote_copy(
            src_ref=source, dst_ref=target, send_sem=send, recv_sem=recv,
            device_id=device, device_id_type=MESH,
        )

    def each(count, body):
        def step(k, carry):
            body(k)
            return carry
        lax.fori_loop(1, count, step, 0)

    def rows_of(index, size):
        return pl.ds(pl.multiple_of(index * size, size), size)

    barrier = pltpu.get_barrier_semaphore()

    def greet(device_of):
        def body(k):
            pl.semaphore_signal(barrier, inc=1, device_id=device_of(k)[1], device_id_type=MESH)
        return body

    each(n_cuts, greet(cut_device))
    each(n_rank, greet(rank_device))

    sketch_parts = split(sketch_ref[...])
    sketched = product(split(two_ref[...].reshape(slices * local, width)), sketch_parts, NN)
    lanes = jnp.concatenate([sketched[n * local : (n + 1) * local] for n in range(slices)], axis=1)
    weights = jnp.concatenate([core_ref[n] for n in range(slices)], axis=1)
    bridge_part[...] = product(split(lanes), split(weights), NT)
    bridge_recv[my_cut] = bridge_part[...]

    pl.semaphore_wait(barrier, n_cuts + n_rank - 2)

    def exchange(source_of, target, phase, device_of, count):
        def body(k):
            peer, device = device_of(k)
            remote(source_of(peer), target, send_sem.at[phase, peer],
                   recv_sem.at[phase, my_cut if device_of is cut_device else my_rank], device).start()
        each(count, body)

    def arrive(target_of, phase, device_of, count):
        def body(k):
            peer, device = device_of(k)
            remote(target_of(peer), target_of(peer), send_sem.at[phase, peer], recv_sem.at[phase, peer], device).wait_recv()
        each(count, body)

    def drain(source, phase, device_of, count):
        def body(k):
            peer, device = device_of(k)
            remote(source, source, send_sem.at[phase, peer], recv_sem.at[phase, peer], device).wait_send()
        each(count, body)

    def total(ref, count):
        value = ref[0]
        for k in range(1, count):
            value = value + ref[k]
        return value

    exchange(lambda peer: bridge_part, bridge_recv.at[my_cut], 0, cut_device, n_cuts)

    one_high[...], one_low[...] = split(one_ref[...].reshape(slices * local, width))
    arrive(lambda peer: bridge_recv.at[peer], 0, cut_device, n_cuts)
    own_bridge = bridge.at[rows_of(my_rank, local), :]
    own_bridge[...] = total(bridge_recv, n_cuts)
    exchange(lambda peer: own_bridge, own_bridge, 1, rank_device, n_rank)
    arrive(lambda peer: bridge.at[rows_of(peer, local), :], 1, rank_device, n_rank)

    own_rows = rows_of(my_rank, local)

    def send_two(n, slot, target_rank):
        @pl.when(my_rank != target_rank)
        def _():
            remote(two_ref.at[n], full_two.at[slot, own_rows, :], two_send.at[n],
                   two_recv.at[slot, my_rank], (my_cut, target_rank)).start()

        @pl.when(my_rank == target_rank)
        def _():
            full_two[slot, own_rows, :] = two_ref[n]

    for slot in range(full):
        def body(k, carry):
            peer, _ = rank_device(k)
            send_two(slot * n_rank + peer, slot, peer)
            return carry
        lax.fori_loop(0, n_rank, body, 0)
    for n in range(full * n_rank, slices):
        send_two(n, full, owner(n))

    def stage(rows_bf, matrix_parts, bridge_ref, index, between):
        base = 2 + 3 * index
        part, recv1, sum1, recv2, sum2, whole = (
            reduce_part.at[index], reduce_recv.at[index], reduce_sum.at[index],
            gather_recv.at[index], gather_sum.at[index], reduced.at[index],
        )
        part[...] = product(rows_bf, matrix_parts, TN)
        recv1[my_cut] = part[rows_of(my_cut, chunk), :]
        exchange(lambda peer: part.at[rows_of(peer, chunk), :], recv1.at[my_cut], base, cut_device, n_cuts)
        between[0]()
        arrive(lambda peer: recv1.at[peer], base, cut_device, n_cuts)
        sum1[...] = total(recv1, n_cuts)
        recv2[my_rank] = sum1[...]
        exchange(lambda peer: sum1, recv2.at[my_rank], base + 1, rank_device, n_rank)
        between[1]()
        arrive(lambda peer: recv2.at[peer], base + 1, rank_device, n_rank)
        own = whole.at[rows_of(my_cut, chunk), :]
        own[...] = total(recv2, n_rank)
        exchange(lambda peer: own, own, base + 2, cut_device, n_cuts)
        between[2]()
        arrive(lambda peer: whole.at[rows_of(peer, chunk), :], base + 2, cut_device, n_cuts)
        gram[...] = exact(whole[...], bridge_ref[...], NN)
        inverse_factor(gram, out_width)

    def nothing():
        pass

    one_parts = (one_high[...], one_low[...])
    first_rows[...] = product(one_parts, split(bridge[...]), NN)

    def land_two():
        for slot in range(slots):
            def wait_rows():
                def body(k):
                    peer, device = rank_device(k)
                    place = full_two.at[slot, rows_of(peer, local), :]
                    remote(place, place, two_send.at[0], two_recv.at[slot, peer], device).wait_recv()
                each(n_rank, body)
            if slot < full:
                wait_rows()
            else:
                pl.when(has_extra(my_rank))(wait_rows)

    stage(split(first_rows[...]), (one_high[...], one_low[...]), bridge, 0, (nothing, nothing, land_two))
    first_carry = split(exact(gram[...], reduced[0], NN))
    first_inverse = split(gram[...] * scale_left)

    for slot in range(slots):
        def project():
            here = slice(slot * out_width, (slot + 1) * out_width)
            block = product(first_carry, split(full_two[slot]), NN)
            projected[here, :] = block
            second_rows[here, :] = product(split(block), sketch_parts, NN)

        def blank():
            here = slice(slot * out_width, (slot + 1) * out_width)
            projected[here, :] = jnp.zeros((out_width, width), F32)
            second_rows[here, :] = jnp.zeros((out_width, out_width), F32)

        if slot < full:
            project()
        else:
            pl.when(has_extra(my_rank))(project)
            pl.when(jnp.logical_not(has_extra(my_rank)))(blank)

    def give_back():
        for slot in range(slots):
            n = slot * n_rank + (my_rank if slot < full else lax.div(my_rank, stride))

            def send_rows():
                returned[n] = second_rows[pl.ds(pl.multiple_of(slot * out_width + my_rank * band, 8), band), :]

                def body(k):
                    peer, device = rank_device(k)
                    source = second_rows.at[pl.ds(pl.multiple_of(slot * out_width + peer * band, 8), band), :]
                    remote(source, returned.at[n], back_send.at[slot, peer], back_recv.at[n], device).start()
                each(n_rank, body)
            if slot < full:
                send_rows()
            else:
                pl.when(has_extra(my_rank))(send_rows)

    def finish_left():
        ortho = product(split(first_rows[...]), first_inverse, NT)
        left_ref[...] = ortho.reshape(slices, local, out_width)

    def land_back():
        for n in range(slices):
            @pl.when(my_rank != owner(n))
            def _():
                remote(returned.at[n], returned.at[n], back_send.at[0, 0], back_recv.at[n],
                       (my_cut, my_rank)).wait_recv()

    stage(split(second_rows[...]), split(projected[...]), sketch_ref, 1, (give_back, finish_left, land_back))
    carry_ref[...] = exact(gram[...], reduced[1], NN)
    flat = returned[...].reshape(slices * band, out_width)
    middle = product(split(flat), split(gram[...] * scale_middle), NT)
    middle_ref[...] = middle.reshape(slices, band, out_width)

    drain(bridge_part, 0, cut_device, n_cuts)
    drain(own_bridge, 1, rank_device, n_rank)
    for index in range(2):
        piece = reduce_sum.at[index]
        drain(piece, 2 + 3 * index, cut_device, n_cuts)
        drain(piece, 3 + 3 * index, rank_device, n_rank)
        drain(piece, 4 + 3 * index, cut_device, n_cuts)
    for n in range(slices):
        @pl.when(my_rank != owner(n))
        def _():
            remote(two_ref.at[n], two_ref.at[n], two_send.at[n], two_recv.at[0, 0], (my_cut, my_rank)).wait_send()
    for slot in range(slots):
        def sent():
            def body(k):
                peer, device = rank_device(k)
                remote(returned.at[0], returned.at[0], back_send.at[slot, peer], back_recv.at[0], device).wait_send()
            each(n_rank, body)
        if slot < full:
            sent()
        else:
            pl.when(has_extra(my_rank))(sent)


def solution(mesh):
    n_cuts, n_rank = mesh.shape["cuts"], mesh.shape["rank"]

    def on_device(core_one, core_two, right_sketch, sketch_core):
        local, slices, width = core_one.shape
        out_width = right_sketch.shape[1]
        band, chunk = out_width // n_rank, out_width // n_cuts
        slots = -(-slices // n_rank)
        rows = local * slices
        scale_left = math.sqrt(local * n_rank * slices * n_cuts)
        scale_middle = math.sqrt(out_width * slices * n_cuts)
        vmem, sems = pltpu.VMEM, pltpu.SemaphoreType.DMA
        widest = max(n_cuts, n_rank)
        left, middle, carry = pl.pallas_call(
            functools.partial(kernel, n_cuts, n_rank, scale_left, scale_middle),
            out_shape=(
                jax.ShapeDtypeStruct((slices, local, out_width), F32),
                jax.ShapeDtypeStruct((slices, band, out_width), F32),
                jax.ShapeDtypeStruct((out_width, width), F32),
            ),
            in_specs=[pl.BlockSpec(memory_space=pltpu.VMEM)] * 4,
            out_specs=(pl.BlockSpec(memory_space=pltpu.VMEM),) * 3,
            scratch_shapes=[
                vmem((rows, width), BF16),
                vmem((rows, width), BF16),
                vmem((local, out_width), F32),
                vmem((n_cuts, local, out_width), F32),
                vmem((width, out_width), F32),
                vmem((rows, out_width), F32),
                vmem((slots, width, width), F32),
                vmem((slots * out_width, width), F32),
                vmem((slots * out_width, out_width), F32),
                vmem((slices, band, out_width), F32),
                vmem((out_width, out_width), F32),
                vmem((2, out_width, width), F32),
                vmem((2, n_cuts, chunk, width), F32),
                vmem((2, chunk, width), F32),
                vmem((2, n_rank, chunk, width), F32),
                vmem((2, chunk, width), F32),
                vmem((2, out_width, width), F32),
                sems((8, widest)),
                sems((8, widest)),
                sems((slices,)),
                sems((slots, n_rank)),
                sems((slots, n_rank)),
                sems((slices,)),
            ],
            compiler_params=pltpu.CompilerParams(
                collective_id=0, has_side_effects=True, vmem_limit_bytes=60 * 1024 * 1024
            ),
        )(
            core_one.transpose(1, 0, 2), core_two.transpose(1, 0, 2),
            right_sketch, sketch_core.transpose(1, 0, 2),
        )
        return left.transpose(1, 0, 2), middle.transpose(1, 0, 2), carry

    placed = (P("rank", "cuts", None), P("rank", "cuts", None), P(), P(None, "cuts", None))
    return jax.shard_map(
        on_device,
        mesh=mesh,
        in_specs=placed,
        out_specs=(P("rank", "cuts", None), P("rank", "cuts", None), P()),
        check_vma=False,
    )
```

```python
import functools
import math

import jax
import jax.numpy as jnp
from jax import lax
from jax.experimental import pallas as pl
from jax.experimental.pallas import tpu as pltpu
from jax.sharding import PartitionSpec as P

MESH = pl.DeviceIdType.MESH
F32 = jnp.float32
BF16 = jnp.bfloat16
NN = (((1,), (0,)), ((), ()))
NT = (((1,), (1,)), ((), ()))
TN = (((0,), (0,)), ((), ()))
PIECES = (0.25, 0.5, 0.7)
EXTRA_PIECE = 3


def split(value):
    high = value.astype(BF16)
    return high, (value - high.astype(F32)).astype(BF16)


def product(left, right, dims):
    (left_high, left_low), (right_high, right_low) = left, right
    dot = functools.partial(lax.dot_general, dimension_numbers=dims, preferred_element_type=F32)
    return dot(left_high, right_high) + (dot(left_high, right_low) + dot(left_low, right_high))


def exact(left, right, dims):
    return lax.dot_general(
        left, right, dims, precision=lax.Precision.HIGHEST, preferred_element_type=F32
    )


def inverse_factor(gram_ref, width):
    blocks = width // 8
    lane = lax.broadcasted_iota(jnp.int32, (8, width), 1)
    row = lax.broadcasted_iota(jnp.int32, (8, width), 0)
    unit = (lane == row).astype(F32)
    block_of = lax.broadcasted_iota(jnp.int32, (blocks, 8, width), 0)
    first_lanes = lax.broadcasted_iota(jnp.int32, (blocks, 8, width), 2) < 8

    def spread(value, i):
        return jnp.broadcast_to(value[i : i + 1, :], (8, width))

    def step(block, carry):
        start = pl.multiple_of(block * 8, 8)
        own = gram_ref[pl.ds(start, 8), :]
        column = [jnp.broadcast_to(own[:, m : m + 1], (8, width)) for m in range(8)]
        entry = [[spread(column[m], i) if m <= i else None for m in range(8)] for i in range(8)]
        replaced = jnp.where(lane < 8, unit, own)
        rows = [spread(replaced, i) for i in range(8)]
        inverse, solved = [], []
        for j in range(8):
            inverse.append(lax.rsqrt(entry[j][j]))
            solved.append(rows[j] * inverse[j])
            for i in range(j + 1, 8):
                entry[i][j] = entry[i][j] * inverse[j]
            for i in range(j + 1, 8):
                rows[i] = rows[i] - entry[i][j] * solved[j]
                for m in range(j + 1, i + 1):
                    entry[i][m] = entry[i][m] - entry[i][j] * entry[m][j]
        back = list(solved)
        for j in reversed(range(8)):
            for i in range(j + 1, 8):
                back[j] = back[j] - entry[i][j] * back[i]
            back[j] = back[j] * inverse[j]
        done = solved[0]
        for j in range(1, 8):
            done = jnp.where(row == j, solved[j], done)
        whole = gram_ref[...].reshape(blocks, 8, width)
        update = jnp.where(first_lanes, 0.0, whole)
        for m in range(8):
            update = update - whole[:, :, m : m + 1] * back[m][None]
        whole = jnp.where(block_of > block, update, jnp.where(block_of == block, done[None], whole))
        gram_ref[...] = pltpu.roll(whole.reshape(width, width), width - 8, 1)
        return carry

    lax.fori_loop(0, blocks, step, 0)
    lower = lax.broadcasted_iota(jnp.int32, (width, width), 0) >= lax.broadcasted_iota(
        jnp.int32, (width, width), 1
    )
    gram_ref[...] = jnp.where(lower, gram_ref[...], 0.0)


def kernel(
    n_cuts, n_rank, scale_left,
    one_ref, two_ref, sketch_ref, core_ref, left_ref, returned_ref, reduced_ref,
    one, two, sketch, core, one_high, one_low,
    bridge_part, bridge_swap, bridge_slices, bridge_half, bridge,
    first_rows, full_two, projected, second_rows, returned, gram,
    part, swapped, half, recv_rank, recv_slice, whole,
    load_sem, swap_send, swap_recv, slice_send, slice_recv, rank_send, rank_recv,
    two_send, two_recv, back_send, back_recv,
):
    slices, local, width = one_ref.shape
    out_width = sketch_ref.shape[1]
    band = out_width // n_rank
    small, half_width = local // 2, width // 2
    n_slices = n_cuts // 2
    side = math.isqrt(n_rank)
    side = side if side * side == n_rank else n_rank
    other = n_rank // side
    my_cut, my_rank = lax.axis_index("cuts"), lax.axis_index("rank")
    my_slice, my_core = lax.div(my_cut, 2), lax.rem(my_cut, 2)
    full, extra = slices // n_rank, slices % n_rank
    stride = max((n_rank - 1) // (extra - 1), 1) if extra > 1 else 1
    slots = full + (1 if extra else 0)

    def has_extra(rank):
        return jnp.logical_and(lax.rem(rank, stride) == 0, lax.div(rank, stride) < extra)

    def away(step, length):
        return min(step, length - step)

    partner = (my_cut + 1 - 2 * my_core, my_rank)
    slice_steps = sorted(range(1, n_slices), key=lambda k: -away(k, n_slices))
    slice_peers = [lax.rem(my_slice + k, n_slices) for k in slice_steps]
    rank_steps = sorted(
        ((i, j) for i in range(side) for j in range(other) if i or j),
        key=lambda t: -(away(t[0], side) + away(t[1], other)),
    )
    rank_peers = [
        lax.rem(lax.div(my_rank, other) + i, side) * other + lax.rem(lax.rem(my_rank, other) + j, other)
        for i, j in rank_steps
    ]

    def slice_device(peer):
        return (peer * 2 + my_core, my_rank)

    def rank_device(peer):
        return (my_cut, peer)

    def remote(source, target, send, recv, device):
        return pltpu.make_async_remote_copy(
            src_ref=source, dst_ref=target, send_sem=send, recv_sem=recv,
            device_id=device, device_id_type=MESH,
        )

    def rows_of(index, size):
        return pl.ds(pl.multiple_of(index * size, size), size)

    barrier = pltpu.get_barrier_semaphore()
    greeted = [partner] + [slice_device(p) for p in slice_peers] + [rank_device(p) for p in rank_peers]
    for device in greeted:
        pl.semaphore_signal(barrier, inc=1, device_id=device, device_id_type=MESH)
    loads = [
        pltpu.make_async_copy(source, target, load_sem.at[k])
        for k, (source, target) in enumerate(
            ((two_ref, two), (sketch_ref, sketch), (core_ref, core), (one_ref, one))
        )
    ]
    for load in loads:
        load.start()
    loads[0].wait()
    loads[1].wait()
    sketch_parts = split(sketch[...])
    sketched = product(split(two[...].reshape(slices * local, width)), sketch_parts, NN)
    loads[2].wait()
    lanes = jnp.concatenate([sketched[n * local : (n + 1) * local] for n in range(slices)], axis=1)
    weights = jnp.concatenate([core[n] for n in range(slices)], axis=1)
    bridge_part[...] = product(split(lanes), split(weights), NT)
    loads[3].wait()
    pl.semaphore_wait(barrier, len(greeted))

    pending = []

    def swap(source, target, phase):
        copy = remote(source, target, swap_send.at[phase], swap_recv.at[phase], partner)
        copy.start()
        pending.append(copy)
        return copy

    def send_slices(source, target, phase):
        for peer in slice_peers:
            copy = remote(source, target, slice_send.at[phase, peer], slice_recv.at[phase, my_slice], slice_device(peer))
            copy.start()
            pending.append(copy)

    def land_slices(target_of, phase):
        for peer in slice_peers:
            place = target_of(peer)
            remote(place, place, slice_send.at[phase, peer], slice_recv.at[phase, peer], slice_device(peer)).wait_recv()

    def send_rank(source_of, target, phase):
        for peer in rank_peers:
            copy = remote(source_of(peer), target, rank_send.at[phase, peer], rank_recv.at[phase, my_rank], rank_device(peer))
            copy.start()
            pending.append(copy)

    def land_rank(target_of, phase):
        for peer in rank_peers:
            place = target_of(peer)
            remote(place, place, rank_send.at[phase, peer], rank_recv.at[phase, peer], rank_device(peer)).wait_recv()

    def total(ref, count):
        value = ref[0]
        for k in range(1, count):
            value = value + ref[k]
        return value

    own_rows = rows_of(my_rank, local)

    def send_two(first, last):
        for peer in rank_peers[first:last]:
            for slot in range(full):
                n = slot * n_rank + peer
                copy = remote(two.at[n], full_two.at[slot, own_rows, :], two_send.at[n], two_recv.at[slot, my_rank], rank_device(peer))
                copy.start()
                pending.append(copy)

    def extra_two(i, action):
        n, target_rank = full * n_rank + i, i * stride

        @pl.when(my_rank != target_rank)
        def _():
            copy = remote(two.at[n], full_two.at[full, own_rows, :], two_send.at[n], two_recv.at[full, my_rank], (my_cut, target_rank))
            action(copy)

    def keep_two():
        for slot in range(full):
            full_two[slot, own_rows, :] = two[slot * n_rank + my_rank]
        for i in range(extra):
            @pl.when(my_rank == i * stride)
            def _():
                full_two[full, own_rows, :] = two[full * n_rank + i]

    def land_two():
        for slot in range(slots):
            def wait_rows():
                for peer in rank_peers:
                    place = full_two.at[slot, rows_of(peer, local), :]
                    remote(place, place, two_send.at[0], two_recv.at[slot, peer], rank_device(peer)).wait_recv()
            if slot < full:
                wait_rows()
            else:
                pl.when(has_extra(my_rank))(wait_rows)

    def pieces(k):
        count = len(rank_peers)
        cuts = [0] + [round(count * part) for part in PIECES] + [count]
        send_two(cuts[k], cuts[k + 1])
        if k == EXTRA_PIECE:
            for i in range(extra):
                extra_two(i, lambda copy: copy.start())

    away_rows = pl.ds(pl.multiple_of((1 - my_core) * small, small), small)
    step = swap(bridge_part.at[away_rows, :], bridge_swap, 0)
    pieces(0)
    keep_two()
    one_high[...], one_low[...] = split(one[...].reshape(slices * local, width))
    step.wait_recv()
    bridge_slices[my_slice] = bridge_part[rows_of(my_core, small), :] + bridge_swap[...]
    send_slices(bridge_slices.at[my_slice], bridge_slices.at[my_slice], 0)
    land_slices(lambda peer: bridge_slices.at[peer], 0)
    own = bridge_half.at[my_core, rows_of(my_rank, small), :]
    own[...] = total(bridge_slices, n_slices)
    send_rank(lambda peer: own, own, 0)
    pieces(1)
    land_rank(lambda peer: bridge_half.at[my_core, rows_of(peer, small), :], 0)
    swap(bridge_half.at[my_core], bridge_half.at[my_core], 1).wait_recv()
    for r in range(n_rank):
        for h in range(2):
            bridge[r * local + h * small : r * local + (h + 1) * small, :] = bridge_half[h, r * small : (r + 1) * small, :]

    def reduce(rows_bf, matrix_parts, index, between):
        both = product(rows_bf, matrix_parts, TN)
        for h in range(2):
            part[index, h] = both[:, h * half_width : (h + 1) * half_width]
        step = swap(part.at[index, 1 - my_core], swapped.at[index], 2 + 2 * index)
        between[0]()
        step.wait_recv()
        half[index] = part[index, my_core] + swapped[index]
        recv_rank[index, my_rank] = half[index, rows_of(my_rank, band), :]
        send_rank(lambda peer: half.at[index, rows_of(peer, band), :], recv_rank.at[index, my_rank], 1 + 2 * index)
        between[1]()
        land_rank(lambda peer: recv_rank.at[index, peer], 1 + 2 * index)
        recv_slice[index, my_slice] = total(recv_rank.at[index], n_rank)
        place = recv_slice.at[index, my_slice]
        send_slices(place, place, 1 + index)
        between[2]()
        land_slices(lambda peer: recv_slice.at[index, peer], 1 + index)
        own = whole.at[index, my_core, rows_of(my_rank, band), :]
        own[...] = total(recv_slice.at[index], n_slices)
        send_rank(lambda peer: own, own, 2 + 2 * index)
        between[3]()
        land_rank(lambda peer: whole.at[index, my_core, rows_of(peer, band), :], 2 + 2 * index)
        swap(whole.at[index, my_core], whole.at[index, my_core], 3 + 2 * index).wait_recv()
        return jnp.concatenate([whole[index, 0], whole[index, 1]], axis=1)

    def nothing():
        pass

    first_rows[...] = product((one_high[...], one_low[...]), split(bridge[...]), NN)
    first_sum = reduce(
        split(first_rows[...]), (one_high[...], one_low[...]), 0,
        (nothing, nothing, lambda: pieces(2), lambda: pieces(3)),
    )
    gram[...] = exact(first_sum, bridge[...], NN)
    inverse_factor(gram, out_width)
    first_carry = split(exact(gram[...], first_sum, NN))
    first_inverse = split(gram[...] * scale_left)
    land_two()

    for slot in range(slots):
        here = slice(slot * out_width, (slot + 1) * out_width)

        def project():
            block = product(first_carry, split(full_two[slot]), NN)
            projected[here, :] = block
            second_rows[here, :] = product(split(block), sketch_parts, NN)

        def blank():
            projected[here, :] = jnp.zeros((out_width, width), F32)
            second_rows[here, :] = jnp.zeros((out_width, out_width), F32)

        if slot < full:
            project()
        else:
            pl.when(has_extra(my_rank))(project)
            pl.when(jnp.logical_not(has_extra(my_rank)))(blank)

    def back(slot, peer):
        n = slot * n_rank + (my_rank if slot < full else lax.div(my_rank, stride))
        source = second_rows.at[pl.ds(pl.multiple_of(slot * out_width + peer * band, 8), band), :]
        return remote(source, returned.at[n], back_send.at[slot, peer], back_recv.at[n], rank_device(peer))

    def give_back():
        for slot in range(slots):
            n = slot * n_rank + (my_rank if slot < full else lax.div(my_rank, stride))

            def send_rows():
                returned[n] = second_rows[pl.ds(pl.multiple_of(slot * out_width + my_rank * band, 8), band), :]
                for peer in rank_peers:
                    back(slot, peer).start()
            if slot < full:
                send_rows()
            else:
                pl.when(has_extra(my_rank))(send_rows)

    def finish_left():
        ortho = product(split(first_rows[...]), first_inverse, NT)
        left_ref[...] = ortho.reshape(slices, local, out_width)

    def land_back():
        for n in range(slices):
            @pl.when(my_rank != (n % n_rank if n < full * n_rank else (n - full * n_rank) * stride))
            def _():
                remote(returned.at[n], returned.at[n], back_send.at[0, 0], back_recv.at[n], partner).wait_recv()
        returned_ref[...] = returned[...]

    reduced_ref[...] = reduce(
        split(second_rows[...]), split(projected[...]), 1, (nothing, nothing, give_back, finish_left),
    )
    land_back()

    for copy in pending:
        copy.wait_send()
    for i in range(extra):
        extra_two(i, lambda copy: copy.wait_send())
    for slot in range(slots):
        def sent():
            for peer in rank_peers:
                back(slot, peer).wait_send()
        if slot < full:
            sent()
        else:
            pl.when(has_extra(my_rank))(sent)


def finish_kernel(scale_middle, reduced_ref, sketch_ref, returned_ref, left_in_ref, left_ref, middle_ref, carry_ref, held, gram, sems):
    into = pltpu.make_async_copy(left_in_ref, held, sems.at[0])
    into.start()
    slices, band, out_width = returned_ref.shape
    gram[...] = exact(reduced_ref[...], sketch_ref[...], NN)
    into.wait()
    out = pltpu.make_async_copy(held, left_ref, sems.at[1])
    out.start()
    inverse_factor(gram, out_width)
    carry_ref[...] = exact(gram[...], reduced_ref[...], NN)
    flat = returned_ref[...].reshape(slices * band, out_width)
    middle = product(split(flat), split(gram[...] * scale_middle), NT)
    middle_ref[...] = middle.reshape(slices, band, out_width)
    out.wait()


def solution(mesh):
    n_cuts, n_rank = mesh.shape["cuts"], mesh.shape["rank"]

    def on_device(core_one, core_two, right_sketch, sketch_core):
        local, slices, width = core_one.shape
        out_width = right_sketch.shape[1]
        band, n_slices = out_width // n_rank, n_cuts // 2
        slots = -(-slices // n_rank)
        rows = local * slices
        scale_left = math.sqrt(local * n_rank * slices * n_cuts)
        scale_middle = math.sqrt(out_width * slices * n_cuts)
        vmem, sems = pltpu.VMEM, pltpu.SemaphoreType.DMA
        any_place, in_vmem = pl.BlockSpec(memory_space=pl.ANY), pl.BlockSpec(memory_space=pltpu.VMEM)
        left, returned, reduced = pl.pallas_call(
            functools.partial(kernel, n_cuts, n_rank, scale_left),
            out_shape=(
                jax.ShapeDtypeStruct((slices, local, out_width), F32),
                jax.ShapeDtypeStruct((slices, band, out_width), F32),
                jax.ShapeDtypeStruct((out_width, width), F32),
            ),
            in_specs=[any_place] * 4,
            out_specs=(in_vmem,) * 3,
            scratch_shapes=[
                vmem((slices, local, width), F32),
                vmem((slices, local, width), F32),
                vmem((width, out_width), F32),
                vmem((slices, out_width, out_width), F32),
                vmem((rows, width), BF16),
                vmem((rows, width), BF16),
                vmem((local, out_width), F32),
                vmem((local // 2, out_width), F32),
                vmem((n_slices, local // 2, out_width), F32),
                vmem((2, width // 2, out_width), F32),
                vmem((width, out_width), F32),
                vmem((rows, out_width), F32),
                vmem((slots, width, width), F32),
                vmem((slots * out_width, width), F32),
                vmem((slots * out_width, out_width), F32),
                vmem((slices, band, out_width), F32),
                vmem((out_width, out_width), F32),
                vmem((2, 2, out_width, width // 2), F32),
                vmem((2, out_width, width // 2), F32),
                vmem((2, out_width, width // 2), F32),
                vmem((2, n_rank, band, width // 2), F32),
                vmem((2, n_slices, band, width // 2), F32),
                vmem((2, 2, out_width, width // 2), F32),
                sems((4,)),
                sems((6,)),
                sems((6,)),
                sems((3, n_slices)),
                sems((3, n_slices)),
                sems((5, n_rank)),
                sems((5, n_rank)),
                sems((slices,)),
                sems((slots, n_rank)),
                sems((slots, n_rank)),
                sems((slices,)),
            ],
            compiler_params=pltpu.CompilerParams(
                collective_id=0, has_side_effects=True, vmem_limit_bytes=60 * 1024 * 1024
            ),
        )(
            core_one.transpose(1, 0, 2), core_two.transpose(1, 0, 2),
            right_sketch, sketch_core.transpose(1, 0, 2),
        )
        left, middle, carry = pl.pallas_call(
            functools.partial(finish_kernel, scale_middle),
            out_shape=(
                jax.ShapeDtypeStruct((slices, local, out_width), F32),
                jax.ShapeDtypeStruct((slices, band, out_width), F32),
                jax.ShapeDtypeStruct((out_width, width), F32),
            ),
            in_specs=[in_vmem] * 3 + [any_place],
            out_specs=(any_place, in_vmem, in_vmem),
            scratch_shapes=[vmem((slices, local, out_width), F32), vmem((out_width, out_width), F32), sems((2,))],
        )(reduced, right_sketch, returned, left)
        return left.transpose(1, 0, 2), middle.transpose(1, 0, 2), carry

    placed = (P("rank", "cuts", None), P("rank", "cuts", None), P(), P(None, "cuts", None))
    return jax.shard_map(
        on_device,
        mesh=mesh,
        in_specs=placed,
        out_specs=(P("rank", "cuts", None), P("rank", "cuts", None), P()),
        check_vma=False,
    )
```

```python
import functools
import math

import jax
import jax.numpy as jnp
from jax import lax
from jax.experimental import pallas as pl
from jax.experimental.pallas import tpu as pltpu
from jax.sharding import PartitionSpec as P

MESH = pl.DeviceIdType.MESH
F32 = jnp.float32
BF16 = jnp.bfloat16
NN = (((1,), (0,)), ((), ()))
NT = (((1,), (1,)), ((), ()))
TN = (((0,), (0,)), ((), ()))
PIECES = (0.35, 0.6, 0.8)
EXTRA_PIECE = 3


def split(value):
    high = value.astype(BF16)
    return high, (value - high.astype(F32)).astype(BF16)


def product(left, right, dims):
    (left_high, left_low), (right_high, right_low) = left, right
    dot = functools.partial(lax.dot_general, dimension_numbers=dims, preferred_element_type=F32)
    return dot(left_high, right_high) + (dot(left_high, right_low) + dot(left_low, right_high))


def exact(left, right, dims):
    return lax.dot_general(
        left, right, dims, precision=lax.Precision.HIGHEST, preferred_element_type=F32
    )


def inverse_factor(gram_ref, rows_ref, columns_ref, width):
    blocks = width // 8
    lane = lax.broadcasted_iota(jnp.int32, (8, width), 1)
    row = lax.broadcasted_iota(jnp.int32, (8, width), 0)
    rest = gram_ref[...].reshape(blocks, 8, width)
    own, rest = rest[0], rest[1:]
    for block in range(blocks):
        base = 8 * block
        last = block + 1 == blocks
        inside = jnp.logical_and(lane >= base, lane < base + 8)
        slot = (block % 2) * 8
        for m in range(8):
            columns_ref[(slot + m) * 8 : (slot + m + 1) * 8, :] = jnp.broadcast_to(own[:, base + m : base + m + 1], (8, width))
        rows_ref[slot : slot + 8, :] = jnp.where(inside, (lane == row + base).astype(F32), own)
        entry = [
            [jnp.broadcast_to(columns_ref[(slot + m) * 8 + i : (slot + m) * 8 + i + 1, :], (8, width)) if m <= i else None for m in range(8)]
            for i in range(8)
        ]
        rows = [jnp.broadcast_to(rows_ref[slot + i : slot + i + 1, :], (8, width)) for i in range(8)]
        if not last:
            ahead = [jnp.broadcast_to(rest[0][:, base + m : base + m + 1], (8, width)) for m in range(8)]
            following = jnp.where(inside, 0.0, rest[0])
        inverse, solved = [], []
        for j in range(8):
            inverse.append(lax.rsqrt(entry[j][j]))
            solved.append(rows[j] * inverse[j])
            for i in range(j + 1, 8):
                entry[i][j] = entry[i][j] * inverse[j]
            for i in range(j + 1, 8):
                rows[i] = rows[i] - entry[i][j] * solved[j]
                for m in range(j + 1, i + 1):
                    entry[i][m] = entry[i][m] - entry[i][j] * entry[m][j]
            if not last:
                factor = ahead[j] * inverse[j]
                following = following - factor * solved[j]
                for m in range(j + 1, 8):
                    ahead[m] = ahead[m] - factor * entry[m][j]
        done = solved[0]
        for j in range(1, 8):
            done = jnp.where(row == j, solved[j], done)
        gram_ref[base : base + 8, :] = jnp.where(lane <= row + base, done, 0.0)
        if last:
            break
        own, rest = following, rest[1:]
        if block + 2 == blocks:
            continue
        back = list(solved)
        for j in reversed(range(8)):
            for i in range(j + 1, 8):
                back[j] = back[j] - entry[i][j] * back[i]
            back[j] = back[j] * inverse[j]
        update = jnp.where(inside[None], 0.0, rest)
        for m in range(8):
            update = update - rest[:, :, base + m : base + m + 1] * back[m][None]
        rest = update


def kernel(
    n_cuts, n_rank, scale_left,
    one_ref, two_ref, sketch_ref, core_ref, left_ref, returned_ref, reduced_ref,
    one, two, sketch, core, one_high, one_low,
    bridge_part, bridge_swap, bridge_slices, bridge_half, bridge,
    first_rows, full_two, projected, second_rows, returned, gram, gram_rows, gram_columns,
    part, swapped, half, recv_rank, recv_slice, whole,
    load_sem, swap_send, swap_recv, slice_send, slice_recv, rank_send, rank_recv,
    two_send, two_recv, back_send, back_recv,
):
    slices, local, width = one_ref.shape
    out_width = sketch_ref.shape[1]
    band = out_width // n_rank
    small, half_width = local // 2, width // 2
    n_slices = n_cuts // 2
    side = math.isqrt(n_rank)
    side = side if side * side == n_rank else n_rank
    other = n_rank // side
    my_cut, my_rank = lax.axis_index("cuts"), lax.axis_index("rank")
    my_slice, my_core = lax.div(my_cut, 2), lax.rem(my_cut, 2)
    full, extra = slices // n_rank, slices % n_rank
    stride = max((n_rank - 1) // (extra - 1), 1) if extra > 1 else 1
    slots = full + (1 if extra else 0)

    square = extra == side and side == other

    def extra_owner(i):
        return i * other + lax.rem(i + 2 * my_core, other) if square else i * stride

    def extra_held(rank):
        return lax.div(rank, other if square else stride)

    def has_extra(rank):
        held = extra_held(rank)
        return jnp.logical_and(held < extra, rank == extra_owner(held))

    def away(step, length):
        return min(step, length - step)

    partner = (my_cut + 1 - 2 * my_core, my_rank)
    slice_steps = sorted(range(1, n_slices), key=lambda k: -away(k, n_slices))
    slice_peers = [lax.rem(my_slice + k, n_slices) for k in slice_steps]
    rank_steps = sorted(
        ((i, j) for i in range(side) for j in range(other) if i or j),
        key=lambda t: -(away(t[0], side) + away(t[1], other)),
    )
    rank_peers = [
        lax.rem(lax.div(my_rank, other) + i, side) * other + lax.rem(lax.rem(my_rank, other) + j, other)
        for i, j in rank_steps
    ]

    def slice_device(peer):
        return (peer * 2 + my_core, my_rank)

    def rank_device(peer):
        return (my_cut, peer)

    def remote(source, target, send, recv, device):
        return pltpu.make_async_remote_copy(
            src_ref=source, dst_ref=target, send_sem=send, recv_sem=recv,
            device_id=device, device_id_type=MESH,
        )

    def rows_of(index, size):
        return pl.ds(pl.multiple_of(index * size, size), size)

    barrier = pltpu.get_barrier_semaphore()
    greeted = [partner] + [slice_device(p) for p in slice_peers] + [rank_device(p) for p in rank_peers]
    for device in greeted:
        pl.semaphore_signal(barrier, inc=1, device_id=device, device_id_type=MESH)
    loads = [
        pltpu.make_async_copy(source, target, load_sem.at[k])
        for k, (source, target) in enumerate(
            ((two_ref, two), (sketch_ref, sketch), (core_ref, core), (one_ref, one))
        )
    ]
    for load in loads:
        load.start()
    loads[0].wait()
    loads[1].wait()
    sketch_parts = split(sketch[...])
    sketched = product(split(two[...].reshape(slices * local, width)), sketch_parts, NN)
    loads[2].wait()
    lanes = jnp.concatenate([sketched[n * local : (n + 1) * local] for n in range(slices)], axis=1)
    weights = jnp.concatenate([core[n] for n in range(slices)], axis=1)
    bridge_part[...] = product(split(lanes), split(weights), NT)
    loads[3].wait()
    pl.semaphore_wait(barrier, len(greeted))

    pending = []

    def swap(source, target, phase):
        copy = remote(source, target, swap_send.at[phase], swap_recv.at[phase], partner)
        copy.start()
        pending.append(copy)
        return copy

    def send_slices(source, target, phase):
        for peer in slice_peers:
            copy = remote(source, target, slice_send.at[phase, peer], slice_recv.at[phase, my_slice], slice_device(peer))
            copy.start()
            pending.append(copy)

    def land_slices(target_of, phase):
        for peer in slice_peers:
            place = target_of(peer)
            remote(place, place, slice_send.at[phase, peer], slice_recv.at[phase, peer], slice_device(peer)).wait_recv()

    def send_rank(source_of, target, phase):
        for peer in rank_peers:
            copy = remote(source_of(peer), target, rank_send.at[phase, peer], rank_recv.at[phase, my_rank], rank_device(peer))
            copy.start()
            pending.append(copy)

    def land_rank(target_of, phase):
        for peer in rank_peers:
            place = target_of(peer)
            remote(place, place, rank_send.at[phase, peer], rank_recv.at[phase, peer], rank_device(peer)).wait_recv()

    def total(ref, count):
        value = ref[0]
        for k in range(1, count):
            value = value + ref[k]
        return value

    own_rows = rows_of(my_rank, local)

    def send_two(first, last):
        for peer in rank_peers[first:last]:
            for slot in range(full):
                n = slot * n_rank + peer
                copy = remote(two.at[n], full_two.at[slot, own_rows, :], two_send.at[n], two_recv.at[slot, my_rank], rank_device(peer))
                copy.start()
                pending.append(copy)

    def extra_two(i, action):
        n, target_rank = full * n_rank + i, extra_owner(i)

        @pl.when(my_rank != target_rank)
        def _():
            copy = remote(two.at[n], full_two.at[full, own_rows, :], two_send.at[n], two_recv.at[full, my_rank], (my_cut, target_rank))
            action(copy)

    def keep_two():
        for slot in range(full):
            full_two[slot, own_rows, :] = two[slot * n_rank + my_rank]
        for i in range(extra):
            @pl.when(my_rank == extra_owner(i))
            def _():
                full_two[full, own_rows, :] = two[full * n_rank + i]

    def land_two():
        for slot in range(slots):
            def wait_rows():
                for peer in rank_peers:
                    place = full_two.at[slot, rows_of(peer, local), :]
                    remote(place, place, two_send.at[0], two_recv.at[slot, peer], rank_device(peer)).wait_recv()
            if slot < full:
                wait_rows()
            else:
                pl.when(has_extra(my_rank))(wait_rows)

    def pieces(k):
        count = len(rank_peers)
        cuts = [0] + [round(count * part) for part in PIECES] + [count]
        send_two(cuts[k], cuts[k + 1])
        if k == EXTRA_PIECE:
            for i in range(extra):
                extra_two(i, lambda copy: copy.start())

    away_rows = pl.ds(pl.multiple_of((1 - my_core) * small, small), small)
    step = swap(bridge_part.at[away_rows, :], bridge_swap, 0)
    pieces(0)
    keep_two()
    one_high[...], one_low[...] = split(one[...].reshape(slices * local, width))
    step.wait_recv()
    bridge_slices[my_slice] = bridge_part[rows_of(my_core, small), :] + bridge_swap[...]
    send_slices(bridge_slices.at[my_slice], bridge_slices.at[my_slice], 0)
    land_slices(lambda peer: bridge_slices.at[peer], 0)
    own = bridge_half.at[my_core, rows_of(my_rank, small), :]
    own[...] = total(bridge_slices, n_slices)
    send_rank(lambda peer: own, own, 0)
    pieces(1)
    land_rank(lambda peer: bridge_half.at[my_core, rows_of(peer, small), :], 0)
    swap(bridge_half.at[my_core], bridge_half.at[my_core], 1).wait_recv()
    for r in range(n_rank):
        for h in range(2):
            bridge[r * local + h * small : r * local + (h + 1) * small, :] = bridge_half[h, r * small : (r + 1) * small, :]

    def reduce(rows_bf, matrix_parts, index, between):
        both = product(rows_bf, matrix_parts, TN)
        for h in range(2):
            part[index, h] = both[:, h * half_width : (h + 1) * half_width]
        step = swap(part.at[index, 1 - my_core], swapped.at[index], 2 + 2 * index)
        between[0]()
        step.wait_recv()
        half[index] = part[index, my_core] + swapped[index]
        recv_rank[index, my_rank] = half[index, rows_of(my_rank, band), :]
        send_rank(lambda peer: half.at[index, rows_of(peer, band), :], recv_rank.at[index, my_rank], 1 + 2 * index)
        between[1]()
        land_rank(lambda peer: recv_rank.at[index, peer], 1 + 2 * index)
        recv_slice[index, my_slice] = total(recv_rank.at[index], n_rank)
        place = recv_slice.at[index, my_slice]
        send_slices(place, place, 1 + index)
        between[2]()
        land_slices(lambda peer: recv_slice.at[index, peer], 1 + index)
        own = whole.at[index, my_core, rows_of(my_rank, band), :]
        own[...] = total(recv_slice.at[index], n_slices)
        send_rank(lambda peer: own, own, 2 + 2 * index)
        between[3]()
        land_rank(lambda peer: whole.at[index, my_core, rows_of(peer, band), :], 2 + 2 * index)
        swap(whole.at[index, my_core], whole.at[index, my_core], 3 + 2 * index).wait_recv()
        return jnp.concatenate([whole[index, 0], whole[index, 1]], axis=1)

    def nothing():
        pass

    first_rows[...] = product((one_high[...], one_low[...]), split(bridge[...]), NN)
    first_sum = reduce(
        split(first_rows[...]), (one_high[...], one_low[...]), 0,
        (nothing, nothing, lambda: pieces(2), lambda: pieces(3)),
    )
    gram[...] = exact(first_sum, bridge[...], NN)
    inverse_factor(gram, gram_rows, gram_columns, out_width)
    first_carry = split(exact(gram[...], first_sum, NN))
    first_inverse = split(gram[...] * scale_left)
    land_two()

    for slot in range(slots):
        here = slice(slot * out_width, (slot + 1) * out_width)

        def project():
            block = product(first_carry, split(full_two[slot]), NN)
            projected[here, :] = block
            second_rows[here, :] = product(split(block), sketch_parts, NN)

        def blank():
            projected[here, :] = jnp.zeros((out_width, width), F32)
            second_rows[here, :] = jnp.zeros((out_width, out_width), F32)

        if slot < full:
            project()
        else:
            pl.when(has_extra(my_rank))(project)
            pl.when(jnp.logical_not(has_extra(my_rank)))(blank)

    def back(slot, peer):
        n = slot * n_rank + (my_rank if slot < full else extra_held(my_rank))
        source = second_rows.at[pl.ds(pl.multiple_of(slot * out_width + peer * band, 8), band), :]
        return remote(source, returned.at[n], back_send.at[slot, peer], back_recv.at[n], rank_device(peer))

    def give_back():
        for slot in range(slots):
            n = slot * n_rank + (my_rank if slot < full else extra_held(my_rank))

            def send_rows():
                returned[n] = second_rows[pl.ds(pl.multiple_of(slot * out_width + my_rank * band, 8), band), :]
                for peer in rank_peers:
                    back(slot, peer).start()
            if slot < full:
                send_rows()
            else:
                pl.when(has_extra(my_rank))(send_rows)

    def finish_left():
        ortho = product(split(first_rows[...]), first_inverse, NT)
        left_ref[...] = ortho.reshape(slices, local, out_width)

    def land_back():
        for n in range(slices):
            @pl.when(my_rank != (n % n_rank if n < full * n_rank else extra_owner(n - full * n_rank)))
            def _():
                remote(returned.at[n], returned.at[n], back_send.at[0, 0], back_recv.at[n], partner).wait_recv()
        returned_ref[...] = returned[...]

    reduced_ref[...] = reduce(
        split(second_rows[...]), split(projected[...]), 1, (nothing, nothing, give_back, finish_left),
    )
    land_back()

    for copy in pending:
        copy.wait_send()
    for i in range(extra):
        extra_two(i, lambda copy: copy.wait_send())
    for slot in range(slots):
        def sent():
            for peer in rank_peers:
                back(slot, peer).wait_send()
        if slot < full:
            sent()
        else:
            pl.when(has_extra(my_rank))(sent)


def finish_kernel(scale_middle, reduced_ref, sketch_ref, returned_ref, left_in_ref, left_ref, middle_ref, carry_ref, held, gram, gram_rows, gram_columns, sems):
    into = pltpu.make_async_copy(left_in_ref, held, sems.at[0])
    into.start()
    slices, band, out_width = returned_ref.shape
    gram[...] = exact(reduced_ref[...], sketch_ref[...], NN)
    into.wait()
    out = pltpu.make_async_copy(held, left_ref, sems.at[1])
    out.start()
    inverse_factor(gram, gram_rows, gram_columns, out_width)
    carry_ref[...] = exact(gram[...], reduced_ref[...], NN)
    flat = returned_ref[...].reshape(slices * band, out_width)
    middle = product(split(flat), split(gram[...] * scale_middle), NT)
    middle_ref[...] = middle.reshape(slices, band, out_width)
    out.wait()


def solution(mesh):
    n_cuts, n_rank = mesh.shape["cuts"], mesh.shape["rank"]

    def on_device(core_one, core_two, right_sketch, sketch_core):
        local, slices, width = core_one.shape
        out_width = right_sketch.shape[1]
        band, n_slices = out_width // n_rank, n_cuts // 2
        slots = -(-slices // n_rank)
        rows = local * slices
        scale_left = math.sqrt(local * n_rank * slices * n_cuts)
        scale_middle = math.sqrt(out_width * slices * n_cuts)
        vmem, sems = pltpu.VMEM, pltpu.SemaphoreType.DMA
        any_place, in_vmem = pl.BlockSpec(memory_space=pl.ANY), pl.BlockSpec(memory_space=pltpu.VMEM)
        left, returned, reduced = pl.pallas_call(
            functools.partial(kernel, n_cuts, n_rank, scale_left),
            out_shape=(
                jax.ShapeDtypeStruct((slices, local, out_width), F32),
                jax.ShapeDtypeStruct((slices, band, out_width), F32),
                jax.ShapeDtypeStruct((out_width, width), F32),
            ),
            in_specs=[any_place] * 4,
            out_specs=(in_vmem,) * 3,
            scratch_shapes=[
                vmem((slices, local, width), F32),
                vmem((slices, local, width), F32),
                vmem((width, out_width), F32),
                vmem((slices, out_width, out_width), F32),
                vmem((rows, width), BF16),
                vmem((rows, width), BF16),
                vmem((local, out_width), F32),
                vmem((local // 2, out_width), F32),
                vmem((n_slices, local // 2, out_width), F32),
                vmem((2, width // 2, out_width), F32),
                vmem((width, out_width), F32),
                vmem((rows, out_width), F32),
                vmem((slots, width, width), F32),
                vmem((slots * out_width, width), F32),
                vmem((slots * out_width, out_width), F32),
                vmem((slices, band, out_width), F32),
                vmem((out_width, out_width), F32),
                vmem((16, out_width), F32),
                vmem((128, out_width), F32),
                vmem((2, 2, out_width, width // 2), F32),
                vmem((2, out_width, width // 2), F32),
                vmem((2, out_width, width // 2), F32),
                vmem((2, n_rank, band, width // 2), F32),
                vmem((2, n_slices, band, width // 2), F32),
                vmem((2, 2, out_width, width // 2), F32),
                sems((4,)),
                sems((6,)),
                sems((6,)),
                sems((3, n_slices)),
                sems((3, n_slices)),
                sems((5, n_rank)),
                sems((5, n_rank)),
                sems((slices,)),
                sems((slots, n_rank)),
                sems((slots, n_rank)),
                sems((slices,)),
            ],
            compiler_params=pltpu.CompilerParams(
                collective_id=0, has_side_effects=True, vmem_limit_bytes=60 * 1024 * 1024
            ),
        )(
            core_one.transpose(1, 0, 2), core_two.transpose(1, 0, 2),
            right_sketch, sketch_core.transpose(1, 0, 2),
        )
        left, middle, carry = pl.pallas_call(
            functools.partial(finish_kernel, scale_middle),
            out_shape=(
                jax.ShapeDtypeStruct((slices, local, out_width), F32),
                jax.ShapeDtypeStruct((slices, band, out_width), F32),
                jax.ShapeDtypeStruct((out_width, width), F32),
            ),
            in_specs=[in_vmem] * 3 + [any_place],
            out_specs=(any_place, in_vmem, in_vmem),
            scratch_shapes=[vmem((slices, local, out_width), F32), vmem((out_width, out_width), F32), vmem((16, out_width), F32), vmem((128, out_width), F32), sems((2,))],
        )(reduced, right_sketch, returned, left)
        return left.transpose(1, 0, 2), middle.transpose(1, 0, 2), carry

    placed = (P("rank", "cuts", None), P("rank", "cuts", None), P(), P(None, "cuts", None))
    return jax.shard_map(
        on_device,
        mesh=mesh,
        in_specs=placed,
        out_specs=(P("rank", "cuts", None), P("rank", "cuts", None), P()),
        check_vma=False,
    )
```

```python
import functools
import math

import jax
import jax.numpy as jnp
from jax import lax
from jax.experimental import pallas as pl
from jax.experimental.pallas import tpu as pltpu
from jax.sharding import PartitionSpec as P

MESH = pl.DeviceIdType.MESH
F32 = jnp.float32
BF16 = jnp.bfloat16
NN = (((1,), (0,)), ((), ()))
NT = (((1,), (1,)), ((), ()))
TN = (((0,), (0,)), ((), ()))
PIECES = (0.4, 0.6, 0.8)
EXTRA_PIECE = 3


def split(value):
    high = value.astype(BF16)
    return high, (value - high.astype(F32)).astype(BF16)


def product(left, right, dims):
    (left_high, left_low), (right_high, right_low) = left, right
    dot = functools.partial(lax.dot_general, dimension_numbers=dims, preferred_element_type=F32)
    return dot(left_high, right_high) + (dot(left_high, right_low) + dot(left_low, right_high))


def inverse_factor(gram_ref, rows_ref, columns_ref, width):
    blocks = width // 8
    lane = lax.broadcasted_iota(jnp.int32, (8, width), 1)
    row = lax.broadcasted_iota(jnp.int32, (8, width), 0)
    rest = gram_ref[...].reshape(blocks, 8, width)
    own, rest = rest[0], rest[1:]
    for block in range(blocks):
        base = 8 * block
        last = block + 1 == blocks
        inside = jnp.logical_and(lane >= base, lane < base + 8)
        slot = (block % 2) * 8
        for m in range(8):
            columns_ref[(slot + m) * 8 : (slot + m + 1) * 8, :] = jnp.broadcast_to(own[:, base + m : base + m + 1], (8, width))
        rows_ref[slot : slot + 8, :] = jnp.where(inside, (lane == row + base).astype(F32), own)
        entry = [
            [jnp.broadcast_to(columns_ref[(slot + m) * 8 + i : (slot + m) * 8 + i + 1, :], (8, width)) if m <= i else None for m in range(8)]
            for i in range(8)
        ]
        rows = [jnp.broadcast_to(rows_ref[slot + i : slot + i + 1, :], (8, width)) for i in range(8)]
        if not last:
            ahead = [jnp.broadcast_to(rest[0][:, base + m : base + m + 1], (8, width)) for m in range(8)]
            following = jnp.where(inside, 0.0, rest[0])
        inverse, solved = [], []
        for j in range(8):
            inverse.append(lax.rsqrt(entry[j][j]))
            solved.append(rows[j] * inverse[j])
            for i in range(j + 1, 8):
                entry[i][j] = entry[i][j] * inverse[j]
            for i in range(j + 1, 8):
                rows[i] = rows[i] - entry[i][j] * solved[j]
                for m in range(j + 1, i + 1):
                    entry[i][m] = entry[i][m] - entry[i][j] * entry[m][j]
            if not last:
                factor = ahead[j] * inverse[j]
                following = following - factor * solved[j]
                for m in range(j + 1, 8):
                    ahead[m] = ahead[m] - factor * entry[m][j]
        done = solved[0]
        for j in range(1, 8):
            done = jnp.where(row == j, solved[j], done)
        gram_ref[base : base + 8, :] = jnp.where(lane <= row + base, done, 0.0)
        if last:
            break
        own, rest = following, rest[1:]
        if block + 2 == blocks:
            continue
        back = list(solved)
        for j in reversed(range(8)):
            for i in range(j + 1, 8):
                back[j] = back[j] - entry[i][j] * back[i]
            back[j] = back[j] * inverse[j]
        update = jnp.where(inside[None], 0.0, rest)
        for m in range(8):
            update = update - rest[:, :, base + m : base + m + 1] * back[m][None]
        rest = update


def kernel(
    n_cuts, n_rank, scale_left,
    one_ref, two_ref, sketch_ref, core_ref, left_ref, returned_ref, reduced_ref,
    one, two, sketch, core, one_high, one_low,
    bridge_part, bridge_swap, bridge_slices, bridge_half, bridge,
    first_rows, full_two, second_rows, returned, left, gram, gram_rows, gram_columns,
    part, swapped, half, recv_rank, recv_slice, whole,
    load_sem, swap_send, swap_recv, slice_send, slice_recv, rank_send, rank_recv,
    two_send, two_recv, back_send, back_recv,
):
    slices, local, width = one_ref.shape
    out_width = sketch_ref.shape[1]
    band = out_width // n_rank
    small, half_width = local // 2, width // 2
    n_slices = n_cuts // 2
    side = math.isqrt(n_rank)
    side = side if side * side == n_rank else n_rank
    other = n_rank // side
    my_cut, my_rank = lax.axis_index("cuts"), lax.axis_index("rank")
    my_slice, my_core = lax.div(my_cut, 2), lax.rem(my_cut, 2)
    full, extra = slices // n_rank, slices % n_rank
    stride = max((n_rank - 1) // (extra - 1), 1) if extra > 1 else 1
    slots = full + (1 if extra else 0)

    square = extra == side and side == other

    def extra_owner(i):
        return i * other + lax.rem(i + 2 * my_core, other) if square else i * stride

    def extra_held(rank):
        return lax.div(rank, other if square else stride)

    def has_extra(rank):
        held = extra_held(rank)
        return jnp.logical_and(held < extra, rank == extra_owner(held))

    def away(step, length):
        return min(step, length - step)

    partner = (my_cut + 1 - 2 * my_core, my_rank)
    slice_steps = sorted(range(1, n_slices), key=lambda k: -away(k, n_slices))
    slice_peers = [lax.rem(my_slice + k, n_slices) for k in slice_steps]
    rank_steps = sorted(
        ((i, j) for i in range(side) for j in range(other) if i or j),
        key=lambda t: -(away(t[0], side) + away(t[1], other)),
    )
    rank_peers = [
        lax.rem(lax.div(my_rank, other) + i, side) * other + lax.rem(lax.rem(my_rank, other) + j, other)
        for i, j in rank_steps
    ]

    def slice_device(peer):
        return (peer * 2 + my_core, my_rank)

    def rank_device(peer):
        return (my_cut, peer)

    def remote(source, target, send, recv, device):
        return pltpu.make_async_remote_copy(
            src_ref=source, dst_ref=target, send_sem=send, recv_sem=recv,
            device_id=device, device_id_type=MESH,
        )

    def rows_of(index, size):
        return pl.ds(pl.multiple_of(index * size, size), size)

    barrier = pltpu.get_barrier_semaphore()
    greeted = [partner] + [slice_device(p) for p in slice_peers] + [rank_device(p) for p in rank_peers]
    for device in greeted:
        pl.semaphore_signal(barrier, inc=1, device_id=device, device_id_type=MESH)
    loads = [
        pltpu.make_async_copy(source, target, load_sem.at[k])
        for k, (source, target) in enumerate(
            ((two_ref, two), (sketch_ref, sketch), (core_ref, core), (one_ref, one))
        )
    ]
    for load in loads:
        load.start()
    loads[0].wait()
    loads[1].wait()
    sketch_parts = split(sketch[...])
    sketched = product(split(two[...].reshape(slices * local, width)), sketch_parts, NN)
    loads[2].wait()
    lanes = jnp.concatenate([sketched[n * local : (n + 1) * local] for n in range(slices)], axis=1)
    weights = jnp.concatenate([core[n] for n in range(slices)], axis=1)
    bridge_part[...] = product(split(lanes), split(weights), NT)
    loads[3].wait()
    pl.semaphore_wait(barrier, len(greeted))

    pending = []

    def swap(source, target, phase):
        copy = remote(source, target, swap_send.at[phase], swap_recv.at[phase], partner)
        copy.start()
        pending.append(copy)
        return copy

    def send_slices(source, target, phase):
        for peer in slice_peers:
            copy = remote(source, target, slice_send.at[phase, peer], slice_recv.at[phase, my_slice], slice_device(peer))
            copy.start()
            pending.append(copy)

    def land_slices(target_of, phase):
        for peer in slice_peers:
            place = target_of(peer)
            remote(place, place, slice_send.at[phase, peer], slice_recv.at[phase, peer], slice_device(peer)).wait_recv()

    def send_rank(source_of, target, phase):
        for peer in rank_peers:
            copy = remote(source_of(peer), target, rank_send.at[phase, peer], rank_recv.at[phase, my_rank], rank_device(peer))
            copy.start()
            pending.append(copy)

    def land_rank(target_of, phase):
        for peer in rank_peers:
            place = target_of(peer)
            remote(place, place, rank_send.at[phase, peer], rank_recv.at[phase, peer], rank_device(peer)).wait_recv()

    def total(ref, count):
        value = ref[0]
        for k in range(1, count):
            value = value + ref[k]
        return value

    own_rows = rows_of(my_rank, local)

    def send_two(first, last):
        for peer in rank_peers[first:last]:
            for slot in range(full):
                n = slot * n_rank + peer
                copy = remote(two.at[n], full_two.at[slot, own_rows, :], two_send.at[n], two_recv.at[slot, my_rank], rank_device(peer))
                copy.start()
                pending.append(copy)

    def extra_two(i, action):
        n, target_rank = full * n_rank + i, extra_owner(i)

        @pl.when(my_rank != target_rank)
        def _():
            copy = remote(two.at[n], full_two.at[full, own_rows, :], two_send.at[n], two_recv.at[full, my_rank], (my_cut, target_rank))
            action(copy)

    def keep_two():
        for slot in range(full):
            full_two[slot, own_rows, :] = two[slot * n_rank + my_rank]
        for i in range(extra):
            @pl.when(my_rank == extra_owner(i))
            def _():
                full_two[full, own_rows, :] = two[full * n_rank + i]

    def land_two(slot):
        for peer in rank_peers:
            place = full_two.at[slot, rows_of(peer, local), :]
            remote(place, place, two_send.at[0], two_recv.at[slot, peer], rank_device(peer)).wait_recv()

    def pieces(k):
        count = len(rank_peers)
        cuts = [0] + [round(count * part) for part in PIECES] + [count]
        send_two(cuts[k], cuts[k + 1])
        if k == EXTRA_PIECE:
            for i in range(extra):
                extra_two(i, lambda copy: copy.start())

    away_rows = pl.ds(pl.multiple_of((1 - my_core) * small, small), small)
    step = swap(bridge_part.at[away_rows, :], bridge_swap, 0)
    pieces(0)
    keep_two()
    one_high[...], one_low[...] = split(one[...].reshape(slices * local, width))
    step.wait_recv()
    bridge_slices[my_slice] = bridge_part[rows_of(my_core, small), :] + bridge_swap[...]
    send_slices(bridge_slices.at[my_slice], bridge_slices.at[my_slice], 0)
    land_slices(lambda peer: bridge_slices.at[peer], 0)
    own = bridge_half.at[my_core, rows_of(my_rank, small), :]
    own[...] = total(bridge_slices, n_slices)
    send_rank(lambda peer: own, own, 0)
    pieces(1)
    land_rank(lambda peer: bridge_half.at[my_core, rows_of(peer, small), :], 0)
    swap(bridge_half.at[my_core], bridge_half.at[my_core], 1).wait_recv()
    for r in range(n_rank):
        for h in range(2):
            bridge[r * local + h * small : r * local + (h + 1) * small, :] = bridge_half[h, r * small : (r + 1) * small, :]

    def put_part(index, rows_parts, matrix_parts, first=True):
        both = product(rows_parts, matrix_parts, TN)
        for h in range(2):
            piece = both[:, h * half_width : (h + 1) * half_width]
            part[index, h] = piece if first else part[index, h] + piece

    def reduce(index, between):
        step = swap(part.at[index, 1 - my_core], swapped.at[index], 2 + 2 * index)
        between[0]()
        step.wait_recv()
        half[index] = part[index, my_core] + swapped[index]
        recv_rank[index, my_rank] = half[index, rows_of(my_rank, band), :]
        send_rank(lambda peer: half.at[index, rows_of(peer, band), :], recv_rank.at[index, my_rank], 1 + 2 * index)
        between[1]()
        land_rank(lambda peer: recv_rank.at[index, peer], 1 + 2 * index)
        recv_slice[index, my_slice] = total(recv_rank.at[index], n_rank)
        place = recv_slice.at[index, my_slice]
        send_slices(place, place, 1 + index)
        between[2]()
        land_slices(lambda peer: recv_slice.at[index, peer], 1 + index)
        own = whole.at[index, my_core, rows_of(my_rank, band), :]
        own[...] = total(recv_slice.at[index], n_slices)
        send_rank(lambda peer: own, own, 2 + 2 * index)
        between[3]()
        land_rank(lambda peer: whole.at[index, my_core, rows_of(peer, band), :], 2 + 2 * index)
        swap(whole.at[index, my_core], whole.at[index, my_core], 3 + 2 * index).wait_recv()
        return jnp.concatenate([whole[index, 0], whole[index, 1]], axis=1)

    def nothing():
        pass

    first_rows[...] = product((one_high[...], one_low[...]), split(bridge[...]), NN)
    put_part(0, split(first_rows[...]), (one_high[...], one_low[...]))
    first_sum = split(reduce(0, (nothing, nothing, lambda: pieces(2), lambda: pieces(3))))
    gram[...] = product(first_sum, split(bridge[...]), NN)
    inverse_factor(gram, gram_rows, gram_columns, out_width)
    first_carry = split(product(split(gram[...]), first_sum, NN))
    first_inverse = split(gram[...] * scale_left)

    for slot in range(slots):
        here = slice(slot * out_width, (slot + 1) * out_width)

        def project():
            land_two(slot)
            block = product(first_carry, split(full_two[slot]), NN)
            parts = split(block)
            rows = product(parts, sketch_parts, NN)
            second_rows[here, :] = rows
            put_part(1, split(rows), parts, slot == 0)

        if slot < full:
            project()
        else:
            pl.when(has_extra(my_rank))(project)

    def back(slot, peer):
        n = slot * n_rank + (my_rank if slot < full else extra_held(my_rank))
        source = second_rows.at[pl.ds(pl.multiple_of(slot * out_width + peer * band, 8), band), :]
        return remote(source, returned.at[n], back_send.at[slot, peer], back_recv.at[n], rank_device(peer))

    def give_back():
        for slot in range(slots):
            n = slot * n_rank + (my_rank if slot < full else extra_held(my_rank))

            def send_rows():
                returned[n] = second_rows[pl.ds(pl.multiple_of(slot * out_width + my_rank * band, 8), band), :]
                for peer in rank_peers:
                    back(slot, peer).start()
            if slot < full:
                send_rows()
            else:
                pl.when(has_extra(my_rank))(send_rows)

    def finish_left():
        ortho = product(split(first_rows[...]), first_inverse, NT)
        left[...] = ortho.reshape(slices, local, out_width)
        outs[0].start()

    def land_back():
        for n in range(slices):
            @pl.when(my_rank != (n % n_rank if n < full * n_rank else extra_owner(n - full * n_rank)))
            def _():
                remote(returned.at[n], returned.at[n], back_send.at[0, 0], back_recv.at[n], partner).wait_recv()
        outs[1].start()

    outs = [
        pltpu.make_async_copy(source, target, load_sem.at[k])
        for k, (source, target) in enumerate(((left, left_ref), (returned, returned_ref)))
    ]

    def land_and_finish():
        land_back()
        finish_left()

    reduced_ref[...] = reduce(1, (nothing, nothing, give_back, land_and_finish))

    for copy in outs:
        copy.wait()
    for copy in pending:
        copy.wait_send()
    for i in range(extra):
        extra_two(i, lambda copy: copy.wait_send())
    for slot in range(slots):
        def sent():
            for peer in rank_peers:
                back(slot, peer).wait_send()
        if slot < full:
            sent()
        else:
            pl.when(has_extra(my_rank))(sent)


def finish_kernel(scale_middle, reduced_ref, sketch_ref, returned_ref, left_in_ref, left_ref, middle_ref, carry_ref, held, rows, gram, gram_rows, gram_columns, sems):
    into = pltpu.make_async_copy(left_in_ref, held, sems.at[0])
    into.start()
    rows_in = pltpu.make_async_copy(returned_ref, rows, sems.at[2])
    rows_in.start()
    slices, band, out_width = returned_ref.shape
    reduced = split(reduced_ref[...])
    gram[...] = product(reduced, split(sketch_ref[...]), NN)
    into.wait()
    out = pltpu.make_async_copy(held, left_ref, sems.at[1])
    out.start()
    inverse_factor(gram, gram_rows, gram_columns, out_width)
    carry_ref[...] = product(split(gram[...]), reduced, NN)
    rows_in.wait()
    flat = rows[...].reshape(slices * band, out_width)
    middle = product(split(flat), split(gram[...] * scale_middle), NT)
    middle_ref[...] = middle.reshape(slices, band, out_width)
    out.wait()


def solution(mesh):
    n_cuts, n_rank = mesh.shape["cuts"], mesh.shape["rank"]

    def on_device(core_one, core_two, right_sketch, sketch_core):
        local, slices, width = core_one.shape
        out_width = right_sketch.shape[1]
        band, n_slices = out_width // n_rank, n_cuts // 2
        slots = -(-slices // n_rank)
        rows = local * slices
        scale_left = math.sqrt(local * n_rank * slices * n_cuts)
        scale_middle = math.sqrt(out_width * slices * n_cuts)
        vmem, sems = pltpu.VMEM, pltpu.SemaphoreType.DMA
        any_place, in_vmem = pl.BlockSpec(memory_space=pl.ANY), pl.BlockSpec(memory_space=pltpu.VMEM)
        left, returned, reduced = pl.pallas_call(
            functools.partial(kernel, n_cuts, n_rank, scale_left),
            out_shape=(
                jax.ShapeDtypeStruct((slices, local, out_width), F32),
                jax.ShapeDtypeStruct((slices, band, out_width), F32),
                jax.ShapeDtypeStruct((out_width, width), F32),
            ),
            in_specs=[any_place] * 4,
            out_specs=(any_place, any_place, in_vmem),
            scratch_shapes=[
                vmem((slices, local, width), F32),
                vmem((slices, local, width), F32),
                vmem((width, out_width), F32),
                vmem((slices, out_width, out_width), F32),
                vmem((rows, width), BF16),
                vmem((rows, width), BF16),
                vmem((local, out_width), F32),
                vmem((local // 2, out_width), F32),
                vmem((n_slices, local // 2, out_width), F32),
                vmem((2, width // 2, out_width), F32),
                vmem((width, out_width), F32),
                vmem((rows, out_width), F32),
                vmem((slots, width, width), F32),
                vmem((slots * out_width, out_width), F32),
                vmem((slices, band, out_width), F32),
                vmem((slices, local, out_width), F32),
                vmem((out_width, out_width), F32),
                vmem((16, out_width), F32),
                vmem((128, out_width), F32),
                vmem((2, 2, out_width, width // 2), F32),
                vmem((2, out_width, width // 2), F32),
                vmem((2, out_width, width // 2), F32),
                vmem((2, n_rank, band, width // 2), F32),
                vmem((2, n_slices, band, width // 2), F32),
                vmem((2, 2, out_width, width // 2), F32),
                sems((4,)),
                sems((6,)),
                sems((6,)),
                sems((3, n_slices)),
                sems((3, n_slices)),
                sems((5, n_rank)),
                sems((5, n_rank)),
                sems((slices,)),
                sems((slots, n_rank)),
                sems((slots, n_rank)),
                sems((slices,)),
            ],
            compiler_params=pltpu.CompilerParams(
                collective_id=0, has_side_effects=True, vmem_limit_bytes=60 * 1024 * 1024
            ),
        )(
            core_one.transpose(1, 0, 2), core_two.transpose(1, 0, 2),
            right_sketch, sketch_core.transpose(1, 0, 2),
        )
        left, middle, carry = pl.pallas_call(
            functools.partial(finish_kernel, scale_middle),
            out_shape=(
                jax.ShapeDtypeStruct((slices, local, out_width), F32),
                jax.ShapeDtypeStruct((slices, band, out_width), F32),
                jax.ShapeDtypeStruct((out_width, width), F32),
            ),
            in_specs=[in_vmem] * 2 + [any_place] * 2,
            out_specs=(any_place, in_vmem, in_vmem),
            scratch_shapes=[
                vmem((slices, local, out_width), F32),
                vmem((slices, band, out_width), F32),
                vmem((out_width, out_width), F32),
                vmem((16, out_width), F32),
                vmem((128, out_width), F32),
                sems((3,)),
            ],
        )(reduced, right_sketch, returned, left)
        return left.transpose(1, 0, 2), middle.transpose(1, 0, 2), carry

    placed = (P("rank", "cuts", None), P("rank", "cuts", None), P(), P(None, "cuts", None))
    return jax.shard_map(
        on_device,
        mesh=mesh,
        in_specs=placed,
        out_specs=(P("rank", "cuts", None), P("rank", "cuts", None), P()),
        check_vma=False,
    )
```

```python
import functools
import math

import jax
import jax.numpy as jnp
from jax import lax
from jax.experimental import pallas as pl
from jax.experimental.pallas import tpu as pltpu
from jax.sharding import PartitionSpec as P

MESH = pl.DeviceIdType.MESH
F32 = jnp.float32
BF16 = jnp.bfloat16
NN = (((1,), (0,)), ((), ()))
NT = (((1,), (1,)), ((), ()))
TN = (((0,), (0,)), ((), ()))
PIECES = (0.4, 0.6, 0.8)
EXTRA_PIECE = 3


def split(value):
    high = value.astype(BF16)
    return high, (value - high.astype(F32)).astype(BF16)


def product(left, right, dims):
    (left_high, left_low), (right_high, right_low) = left, right
    dot = functools.partial(lax.dot_general, dimension_numbers=dims, preferred_element_type=F32)
    return dot(left_high, right_high) + (dot(left_high, right_low) + dot(left_low, right_high))


def inverse_factor(gram_ref, rows_ref, columns_ref, width):
    blocks = width // 8
    lane = lax.broadcasted_iota(jnp.int32, (8, width), 1)
    row = lax.broadcasted_iota(jnp.int32, (8, width), 0)
    rest = gram_ref[...].reshape(blocks, 8, width)
    own, rest = rest[0], rest[1:]
    for block in range(blocks):
        base = 8 * block
        last = block + 1 == blocks
        inside = jnp.logical_and(lane >= base, lane < base + 8)
        slot = (block % 2) * 8
        for m in range(8):
            columns_ref[(slot + m) * 8 : (slot + m + 1) * 8, :] = jnp.broadcast_to(own[:, base + m : base + m + 1], (8, width))
        rows_ref[slot : slot + 8, :] = jnp.where(inside, (lane == row + base).astype(F32), own)
        entry = [
            [jnp.broadcast_to(columns_ref[(slot + m) * 8 + i : (slot + m) * 8 + i + 1, :], (8, width)) if m <= i else None for m in range(8)]
            for i in range(8)
        ]
        rows = [jnp.broadcast_to(rows_ref[slot + i : slot + i + 1, :], (8, width)) for i in range(8)]
        if not last:
            ahead = [jnp.broadcast_to(rest[0][:, base + m : base + m + 1], (8, width)) for m in range(8)]
            following = jnp.where(inside, 0.0, rest[0])
        inverse, solved = [], []
        for j in range(8):
            inverse.append(lax.rsqrt(entry[j][j]))
            solved.append(rows[j] * inverse[j])
            for i in range(j + 1, 8):
                entry[i][j] = entry[i][j] * inverse[j]
            for i in range(j + 1, 8):
                rows[i] = rows[i] - entry[i][j] * solved[j]
                for m in range(j + 1, i + 1):
                    entry[i][m] = entry[i][m] - entry[i][j] * entry[m][j]
            if not last:
                factor = ahead[j] * inverse[j]
                following = following - factor * solved[j]
                for m in range(j + 1, 8):
                    ahead[m] = ahead[m] - factor * entry[m][j]
        done = solved[0]
        for j in range(1, 8):
            done = jnp.where(row == j, solved[j], done)
        gram_ref[base : base + 8, :] = jnp.where(lane <= row + base, done, 0.0)
        if last:
            break
        own, rest = following, rest[1:]
        if block + 2 == blocks:
            continue
        back = list(solved)
        for j in reversed(range(8)):
            for i in range(j + 1, 8):
                back[j] = back[j] - entry[i][j] * back[i]
            back[j] = back[j] * inverse[j]
        update = jnp.where(inside[None], 0.0, rest)
        for m in range(8):
            update = update - rest[:, :, base + m : base + m + 1] * back[m][None]
        rest = update


def kernel(
    n_cuts, n_rank, scale_left,
    one_ref, two_ref, sketch_ref, core_ref, left_ref, returned_ref, reduced_ref, gram_ref,
    one, two, sketch, core, one_high, one_low, square_high, square_low,
    bridge_part, bridge_swap, bridge_slices, bridge_half, bridge,
    first_rows, full_two, second_rows, returned, left, gram, gram_rows, gram_columns,
    part, swapped, half, recv_rank, recv_slice, whole,
    load_sem, swap_send, swap_recv, slice_send, slice_recv, rank_send, rank_recv,
    two_send, two_recv, back_send, back_recv,
):
    slices, local, width = one_ref.shape
    out_width = sketch_ref.shape[1]
    band = out_width // n_rank
    small, half_width = local // 2, width // 2
    n_slices = n_cuts // 2
    side = math.isqrt(n_rank)
    side = side if side * side == n_rank else n_rank
    other = n_rank // side
    my_cut, my_rank = lax.axis_index("cuts"), lax.axis_index("rank")
    my_slice, my_core = lax.div(my_cut, 2), lax.rem(my_cut, 2)
    full, extra = slices // n_rank, slices % n_rank
    stride = max((n_rank - 1) // (extra - 1), 1) if extra > 1 else 1
    slots = full + (1 if extra else 0)

    square = extra == side and side == other

    def extra_owner(i):
        return i * other + lax.rem(i + 2 * my_core, other) if square else i * stride

    def extra_held(rank):
        return lax.div(rank, other if square else stride)

    def has_extra(rank):
        held = extra_held(rank)
        return jnp.logical_and(held < extra, rank == extra_owner(held))

    def away(step, length):
        return min(step, length - step)

    partner = (my_cut + 1 - 2 * my_core, my_rank)
    slice_steps = sorted(range(1, n_slices), key=lambda k: -away(k, n_slices))
    slice_peers = [lax.rem(my_slice + k, n_slices) for k in slice_steps]
    rank_steps = sorted(
        ((i, j) for i in range(side) for j in range(other) if i or j),
        key=lambda t: -(away(t[0], side) + away(t[1], other)),
    )
    rank_peers = [
        lax.rem(lax.div(my_rank, other) + i, side) * other + lax.rem(lax.rem(my_rank, other) + j, other)
        for i, j in rank_steps
    ]

    def slice_device(peer):
        return (peer * 2 + my_core, my_rank)

    def rank_device(peer):
        return (my_cut, peer)

    def remote(source, target, send, recv, device):
        return pltpu.make_async_remote_copy(
            src_ref=source, dst_ref=target, send_sem=send, recv_sem=recv,
            device_id=device, device_id_type=MESH,
        )

    def rows_of(index, size):
        return pl.ds(pl.multiple_of(index * size, size), size)

    barrier = pltpu.get_barrier_semaphore()
    greeted = [partner] + [slice_device(p) for p in slice_peers] + [rank_device(p) for p in rank_peers]
    for device in greeted:
        pl.semaphore_signal(barrier, inc=1, device_id=device, device_id_type=MESH)
    loads = [
        pltpu.make_async_copy(source, target, load_sem.at[k])
        for k, (source, target) in enumerate(
            ((two_ref, two), (sketch_ref, sketch), (core_ref, core), (one_ref, one))
        )
    ]
    for load in loads:
        load.start()
    loads[0].wait()
    loads[1].wait()
    sketch_parts = split(sketch[...])
    sketched = product(split(two[...].reshape(slices * local, width)), sketch_parts, NN)
    loads[2].wait()
    lanes = jnp.concatenate([sketched[n * local : (n + 1) * local] for n in range(slices)], axis=1)
    weights = jnp.concatenate([core[n] for n in range(slices)], axis=1)
    bridge_part[...] = product(split(lanes), split(weights), NT)
    loads[3].wait()
    pl.semaphore_wait(barrier, len(greeted))

    pending = []

    def swap(source, target, phase):
        copy = remote(source, target, swap_send.at[phase], swap_recv.at[phase], partner)
        copy.start()
        pending.append(copy)
        return copy

    def send_slices(source, target, phase):
        for peer in slice_peers:
            copy = remote(source, target, slice_send.at[phase, peer], slice_recv.at[phase, my_slice], slice_device(peer))
            copy.start()
            pending.append(copy)

    def land_slices(target_of, phase):
        for peer in slice_peers:
            place = target_of(peer)
            remote(place, place, slice_send.at[phase, peer], slice_recv.at[phase, peer], slice_device(peer)).wait_recv()

    def send_rank(source_of, target, phase):
        for peer in rank_peers:
            copy = remote(source_of(peer), target, rank_send.at[phase, peer], rank_recv.at[phase, my_rank], rank_device(peer))
            copy.start()
            pending.append(copy)

    def land_rank(target_of, phase):
        for peer in rank_peers:
            place = target_of(peer)
            remote(place, place, rank_send.at[phase, peer], rank_recv.at[phase, peer], rank_device(peer)).wait_recv()

    def total(ref, count):
        value = ref[0]
        for k in range(1, count):
            value = value + ref[k]
        return value

    own_rows = rows_of(my_rank, local)

    def send_two(first, last):
        for peer in rank_peers[first:last]:
            for slot in range(full):
                n = slot * n_rank + peer
                copy = remote(two.at[n], full_two.at[slot, own_rows, :], two_send.at[n], two_recv.at[slot, my_rank], rank_device(peer))
                copy.start()
                pending.append(copy)

    def extra_two(i, action):
        n, target_rank = full * n_rank + i, extra_owner(i)

        @pl.when(my_rank != target_rank)
        def _():
            copy = remote(two.at[n], full_two.at[full, own_rows, :], two_send.at[n], two_recv.at[full, my_rank], (my_cut, target_rank))
            action(copy)

    def keep_two():
        for slot in range(full):
            full_two[slot, own_rows, :] = two[slot * n_rank + my_rank]
        for i in range(extra):
            @pl.when(my_rank == extra_owner(i))
            def _():
                full_two[full, own_rows, :] = two[full * n_rank + i]

    def land_two(slot):
        for peer in rank_peers:
            place = full_two.at[slot, rows_of(peer, local), :]
            remote(place, place, two_send.at[0], two_recv.at[slot, peer], rank_device(peer)).wait_recv()

    def pieces(k):
        count = len(rank_peers)
        cuts = [0] + [round(count * part) for part in PIECES] + [count]
        send_two(cuts[k], cuts[k + 1])
        if k == EXTRA_PIECE:
            for i in range(extra):
                extra_two(i, lambda copy: copy.start())

    away_rows = pl.ds(pl.multiple_of((1 - my_core) * small, small), small)
    step = swap(bridge_part.at[away_rows, :], bridge_swap, 0)
    pieces(0)
    keep_two()
    step.wait_recv()
    bridge_slices[my_slice] = bridge_part[rows_of(my_core, small), :] + bridge_swap[...]
    send_slices(bridge_slices.at[my_slice], bridge_slices.at[my_slice], 0)
    one_high[...], one_low[...] = split(one[...].reshape(slices * local, width))
    one_parts = (one_high[...], one_low[...])
    square_high[...], square_low[...] = split(product(one_parts, one_parts, TN))
    land_slices(lambda peer: bridge_slices.at[peer], 0)
    own = bridge_half.at[my_core, rows_of(my_rank, small), :]
    own[...] = total(bridge_slices, n_slices)
    send_rank(lambda peer: own, own, 0)
    pieces(1)
    land_rank(lambda peer: bridge_half.at[my_core, rows_of(peer, small), :], 0)
    swap(bridge_half.at[my_core], bridge_half.at[my_core], 1).wait_recv()
    for r in range(n_rank):
        for h in range(2):
            bridge[r * local + h * small : r * local + (h + 1) * small, :] = bridge_half[h, r * small : (r + 1) * small, :]

    def put_part(index, rows_parts, matrix_parts, first=True):
        both = product(rows_parts, matrix_parts, TN)
        for h in range(2):
            piece = both[:, h * half_width : (h + 1) * half_width]
            part[index, h] = piece if first else part[index, h] + piece

    def reduce(index, between):
        step = swap(part.at[index, 1 - my_core], swapped.at[index], 2 + 2 * index)
        between[0]()
        step.wait_recv()
        half[index] = part[index, my_core] + swapped[index]
        recv_rank[index, my_rank] = half[index, rows_of(my_rank, band), :]
        send_rank(lambda peer: half.at[index, rows_of(peer, band), :], recv_rank.at[index, my_rank], 1 + 2 * index)
        between[1]()
        land_rank(lambda peer: recv_rank.at[index, peer], 1 + 2 * index)
        recv_slice[index, my_slice] = total(recv_rank.at[index], n_rank)
        place = recv_slice.at[index, my_slice]
        send_slices(place, place, 1 + index)
        between[2]()
        land_slices(lambda peer: recv_slice.at[index, peer], 1 + index)
        own = whole.at[index, my_core, rows_of(my_rank, band), :]
        own[...] = total(recv_slice.at[index], n_slices)
        send_rank(lambda peer: own, own, 2 + 2 * index)
        between[3]()
        land_rank(lambda peer: whole.at[index, my_core, rows_of(peer, band), :], 2 + 2 * index)
        swap(whole.at[index, my_core], whole.at[index, my_core], 3 + 2 * index).wait_recv()
        return jnp.concatenate([whole[index, 0], whole[index, 1]], axis=1)

    def nothing():
        pass

    def rows_one():
        first_rows[...] = product((one_high[...], one_low[...]), split(bridge[...]), NN)

    put_part(0, split(bridge[...]), (square_high[...], square_low[...]))
    first_sum = split(reduce(0, (nothing, rows_one, lambda: pieces(2), lambda: pieces(3))))
    gram[...] = product(first_sum, split(bridge[...]), NN)
    inverse_factor(gram, gram_rows, gram_columns, out_width)
    first_carry = split(product(split(gram[...]), first_sum, NN))
    first_inverse = split(gram[...] * scale_left)

    for slot in range(slots):
        here = slice(slot * out_width, (slot + 1) * out_width)

        def project():
            land_two(slot)
            block = product(first_carry, split(full_two[slot]), NN)
            parts = split(block)
            rows = product(parts, sketch_parts, NN)
            second_rows[here, :] = rows
            put_part(1, split(rows), parts, slot == 0)

        if slot < full:
            project()
        else:
            pl.when(has_extra(my_rank))(project)

    def back(slot, peer):
        n = slot * n_rank + (my_rank if slot < full else extra_held(my_rank))
        source = second_rows.at[pl.ds(pl.multiple_of(slot * out_width + peer * band, 8), band), :]
        return remote(source, returned.at[n], back_send.at[slot, peer], back_recv.at[n], rank_device(peer))

    def give_back():
        for slot in range(slots):
            n = slot * n_rank + (my_rank if slot < full else extra_held(my_rank))

            def send_rows():
                returned[n] = second_rows[pl.ds(pl.multiple_of(slot * out_width + my_rank * band, 8), band), :]
                for peer in rank_peers:
                    back(slot, peer).start()
            if slot < full:
                send_rows()
            else:
                pl.when(has_extra(my_rank))(send_rows)

    def finish_left():
        ortho = product(split(first_rows[...]), first_inverse, NT)
        left[...] = ortho.reshape(slices, local, out_width)
        outs[0].start()

    def land_back():
        for n in range(slices):
            @pl.when(my_rank != (n % n_rank if n < full * n_rank else extra_owner(n - full * n_rank)))
            def _():
                remote(returned.at[n], returned.at[n], back_send.at[0, 0], back_recv.at[n], partner).wait_recv()
        outs[1].start()

    outs = [
        pltpu.make_async_copy(source, target, load_sem.at[k])
        for k, (source, target) in enumerate(((left, left_ref), (returned, returned_ref)))
    ]

    def land_and_finish():
        land_back()
        finish_left()

    second_sum = reduce(1, (nothing, nothing, give_back, land_and_finish))
    outs.append(pltpu.make_async_copy(whole.at[1], reduced_ref, load_sem.at[2]))
    outs[2].start()
    gram_ref[...] = product(split(second_sum), sketch_parts, NN)

    for copy in outs:
        copy.wait()
    for copy in pending:
        copy.wait_send()
    for i in range(extra):
        extra_two(i, lambda copy: copy.wait_send())
    for slot in range(slots):
        def sent():
            for peer in rank_peers:
                back(slot, peer).wait_send()
        if slot < full:
            sent()
        else:
            pl.when(has_extra(my_rank))(sent)


def finish_kernel(
    scale_middle, gram_ref, reduced_ref, returned_ref, left_in_ref, left_ref, middle_ref, carry_ref,
    reduced, rows, held, gram, gram_rows, gram_columns, sems,
):
    loads = [
        pltpu.make_async_copy(source, target, sems.at[k])
        for k, (source, target) in enumerate(((left_in_ref, held), (returned_ref, rows), (reduced_ref, reduced)))
    ]
    for load in loads:
        load.start()
    slices, band, out_width = rows.shape
    gram[...] = gram_ref[...]
    inverse_factor(gram, gram_rows, gram_columns, out_width)
    loads[0].wait()
    out = pltpu.make_async_copy(held, left_ref, sems.at[3])
    out.start()
    inverse = split(gram[...])
    loads[2].wait()
    carry_ref[...] = product(inverse, split(jnp.concatenate([reduced[0], reduced[1]], axis=1)), NN)
    loads[1].wait()
    flat = rows[...].reshape(slices * band, out_width)
    middle = product(split(flat), split(gram[...] * scale_middle), NT)
    middle_ref[...] = middle.reshape(slices, band, out_width)
    out.wait()


def solution(mesh):
    n_cuts, n_rank = mesh.shape["cuts"], mesh.shape["rank"]

    def on_device(core_one, core_two, right_sketch, sketch_core):
        local, slices, width = core_one.shape
        out_width = right_sketch.shape[1]
        band, n_slices = out_width // n_rank, n_cuts // 2
        slots = -(-slices // n_rank)
        rows = local * slices
        scale_left = math.sqrt(local * n_rank * slices * n_cuts)
        scale_middle = math.sqrt(out_width * slices * n_cuts)
        vmem, sems = pltpu.VMEM, pltpu.SemaphoreType.DMA
        any_place, in_vmem = pl.BlockSpec(memory_space=pl.ANY), pl.BlockSpec(memory_space=pltpu.VMEM)
        left, returned, reduced, gram = pl.pallas_call(
            functools.partial(kernel, n_cuts, n_rank, scale_left),
            out_shape=(
                jax.ShapeDtypeStruct((slices, local, out_width), F32),
                jax.ShapeDtypeStruct((slices, band, out_width), F32),
                jax.ShapeDtypeStruct((2, out_width, width // 2), F32),
                jax.ShapeDtypeStruct((out_width, out_width), F32),
            ),
            in_specs=[any_place] * 4,
            out_specs=(any_place,) * 3 + (in_vmem,),
            scratch_shapes=[
                vmem((slices, local, width), F32),
                vmem((slices, local, width), F32),
                vmem((width, out_width), F32),
                vmem((slices, out_width, out_width), F32),
                vmem((rows, width), BF16),
                vmem((rows, width), BF16),
                vmem((width, width), BF16),
                vmem((width, width), BF16),
                vmem((local, out_width), F32),
                vmem((local // 2, out_width), F32),
                vmem((n_slices, local // 2, out_width), F32),
                vmem((2, width // 2, out_width), F32),
                vmem((width, out_width), F32),
                vmem((rows, out_width), F32),
                vmem((slots, width, width), F32),
                vmem((slots * out_width, out_width), F32),
                vmem((slices, band, out_width), F32),
                vmem((slices, local, out_width), F32),
                vmem((out_width, out_width), F32),
                vmem((16, out_width), F32),
                vmem((128, out_width), F32),
                vmem((2, 2, out_width, width // 2), F32),
                vmem((2, out_width, width // 2), F32),
                vmem((2, out_width, width // 2), F32),
                vmem((2, n_rank, band, width // 2), F32),
                vmem((2, n_slices, band, width // 2), F32),
                vmem((2, 2, out_width, width // 2), F32),
                sems((4,)),
                sems((6,)),
                sems((6,)),
                sems((3, n_slices)),
                sems((3, n_slices)),
                sems((5, n_rank)),
                sems((5, n_rank)),
                sems((slices,)),
                sems((slots, n_rank)),
                sems((slots, n_rank)),
                sems((slices,)),
            ],
            compiler_params=pltpu.CompilerParams(
                collective_id=0, has_side_effects=True, vmem_limit_bytes=60 * 1024 * 1024
            ),
        )(
            core_one.transpose(1, 0, 2), core_two.transpose(1, 0, 2),
            right_sketch, sketch_core.transpose(1, 0, 2),
        )
        left, middle, carry = pl.pallas_call(
            functools.partial(finish_kernel, scale_middle),
            out_shape=(
                jax.ShapeDtypeStruct((slices, local, out_width), F32),
                jax.ShapeDtypeStruct((slices, band, out_width), F32),
                jax.ShapeDtypeStruct((out_width, width), F32),
            ),
            in_specs=[in_vmem] + [any_place] * 3,
            out_specs=(any_place, in_vmem, in_vmem),
            scratch_shapes=[
                vmem((2, out_width, width // 2), F32),
                vmem((slices, band, out_width), F32),
                vmem((slices, local, out_width), F32),
                vmem((out_width, out_width), F32),
                vmem((16, out_width), F32),
                vmem((128, out_width), F32),
                sems((4,)),
            ],
        )(gram, reduced, returned, left)
        return left.transpose(1, 0, 2), middle.transpose(1, 0, 2), carry

    placed = (P("rank", "cuts", None), P("rank", "cuts", None), P(), P(None, "cuts", None))
    return jax.shard_map(
        on_device,
        mesh=mesh,
        in_specs=placed,
        out_specs=(P("rank", "cuts", None), P("rank", "cuts", None), P()),
        check_vma=False,
    )
```

```python
import functools
import math

import jax
import jax.numpy as jnp
from jax import lax
from jax.experimental import pallas as pl
from jax.experimental.pallas import tpu as pltpu
from jax.sharding import PartitionSpec as P

MESH = pl.DeviceIdType.MESH
F32 = jnp.float32
BF16 = jnp.bfloat16
NN = (((1,), (0,)), ((), ()))
NT = (((1,), (1,)), ((), ()))
TN = (((0,), (0,)), ((), ()))
PIECES = (0.4, 0.6, 0.8)
EXTRA_PIECE = 3


def split(value):
    high = value.astype(BF16)
    return high, (value - high.astype(F32)).astype(BF16)


def product(left, right, dims):
    (left_high, left_low), (right_high, right_low) = left, right
    dot = functools.partial(lax.dot_general, dimension_numbers=dims, preferred_element_type=F32)
    return dot(left_high, right_high) + (dot(left_high, right_low) + dot(left_low, right_high))


def inverse_factor(gram_ref, rows_ref, columns_ref, width):
    blocks = width // 8
    lane = lax.broadcasted_iota(jnp.int32, (8, width), 1)
    row = lax.broadcasted_iota(jnp.int32, (8, width), 0)
    rest = gram_ref[...].reshape(blocks, 8, width)
    own, rest = rest[0], rest[1:]
    for block in range(blocks):
        base = 8 * block
        last = block + 1 == blocks
        inside = jnp.logical_and(lane >= base, lane < base + 8)
        slot = (block % 2) * 8
        for m in range(8):
            columns_ref[(slot + m) * 8 : (slot + m + 1) * 8, :] = jnp.broadcast_to(own[:, base + m : base + m + 1], (8, width))
        rows_ref[slot : slot + 8, :] = jnp.where(inside, (lane == row + base).astype(F32), own)
        entry = [
            [jnp.broadcast_to(columns_ref[(slot + m) * 8 + i : (slot + m) * 8 + i + 1, :], (8, width)) if m <= i else None for m in range(8)]
            for i in range(8)
        ]
        rows = [jnp.broadcast_to(rows_ref[slot + i : slot + i + 1, :], (8, width)) for i in range(8)]
        if not last:
            ahead = [jnp.broadcast_to(rest[0][:, base + m : base + m + 1], (8, width)) for m in range(8)]
            following = jnp.where(inside, 0.0, rest[0])
        inverse, solved = [], []
        for j in range(8):
            inverse.append(lax.rsqrt(entry[j][j]))
            solved.append(rows[j] * inverse[j])
            for i in range(j + 1, 8):
                entry[i][j] = entry[i][j] * inverse[j]
            for i in range(j + 1, 8):
                rows[i] = rows[i] - entry[i][j] * solved[j]
                for m in range(j + 1, i + 1):
                    entry[i][m] = entry[i][m] - entry[i][j] * entry[m][j]
            if not last:
                factor = ahead[j] * inverse[j]
                following = following - factor * solved[j]
                for m in range(j + 1, 8):
                    ahead[m] = ahead[m] - factor * entry[m][j]
        done = solved[0]
        for j in range(1, 8):
            done = jnp.where(row == j, solved[j], done)
        gram_ref[base : base + 8, :] = jnp.where(lane <= row + base, done, 0.0)
        if last:
            break
        own, rest = following, rest[1:]
        if block + 2 == blocks:
            continue
        back = list(solved)
        for j in reversed(range(8)):
            for i in range(j + 1, 8):
                back[j] = back[j] - entry[i][j] * back[i]
            back[j] = back[j] * inverse[j]
        update = jnp.where(inside[None], 0.0, rest)
        for m in range(8):
            update = update - rest[:, :, base + m : base + m + 1] * back[m][None]
        rest = update


def kernel(
    n_cuts, n_rank, scale_left,
    one_ref, two_ref, sketch_ref, core_ref, left_ref, returned_ref, reduced_ref, gram_ref,
    one, two, sketch, core, one_high, one_low, square_high, square_low,
    bridge_part, bridge_swap, bridge_slices, bridge_half, bridge,
    first_rows, full_two, second_rows, returned, left, gram, gram_rows, gram_columns,
    part, swapped, half, recv_rank, recv_slice, whole,
    load_sem, swap_send, swap_recv, slice_send, slice_recv, rank_send, rank_recv,
    two_send, two_recv, back_send, back_recv,
):
    slices, local, width = one_ref.shape
    out_width = sketch_ref.shape[1]
    band = out_width // n_rank
    small, half_width = local // 2, width // 2
    n_slices = n_cuts // 2
    side = math.isqrt(n_rank)
    side = side if side * side == n_rank else n_rank
    other = n_rank // side
    my_cut, my_rank = lax.axis_index("cuts"), lax.axis_index("rank")
    my_slice, my_core = lax.div(my_cut, 2), lax.rem(my_cut, 2)
    full, extra = slices // n_rank, slices % n_rank
    stride = max((n_rank - 1) // (extra - 1), 1) if extra > 1 else 1
    slots = full + (1 if extra else 0)

    square = extra == side and side == other

    def extra_owner(i):
        return i * other + lax.rem(i + 2 * my_core, other) if square else i * stride

    def extra_held(rank):
        return lax.div(rank, other if square else stride)

    def has_extra(rank):
        held = extra_held(rank)
        return jnp.logical_and(held < extra, rank == extra_owner(held))

    def away(step, length):
        return min(step, length - step)

    partner = (my_cut + 1 - 2 * my_core, my_rank)
    slice_steps = sorted(range(1, n_slices), key=lambda k: -away(k, n_slices))
    slice_peers = [lax.rem(my_slice + k, n_slices) for k in slice_steps]
    rank_steps = sorted(
        ((i, j) for i in range(side) for j in range(other) if i or j),
        key=lambda t: -(away(t[0], side) + away(t[1], other)),
    )
    rank_peers = [
        lax.rem(lax.div(my_rank, other) + i, side) * other + lax.rem(lax.rem(my_rank, other) + j, other)
        for i, j in rank_steps
    ]

    def slice_device(peer):
        return (peer * 2 + my_core, my_rank)

    def rank_device(peer):
        return (my_cut, peer)

    def remote(source, target, send, recv, device):
        return pltpu.make_async_remote_copy(
            src_ref=source, dst_ref=target, send_sem=send, recv_sem=recv,
            device_id=device, device_id_type=MESH,
        )

    def rows_of(index, size):
        return pl.ds(pl.multiple_of(index * size, size), size)

    barrier = pltpu.get_barrier_semaphore()
    greeted = [partner] + [slice_device(p) for p in slice_peers] + [rank_device(p) for p in rank_peers]
    for device in greeted:
        pl.semaphore_signal(barrier, inc=1, device_id=device, device_id_type=MESH)
    loads = [
        pltpu.make_async_copy(source, target, load_sem.at[k])
        for k, (source, target) in enumerate(
            ((two_ref, two), (sketch_ref, sketch), (core_ref, core), (one_ref, one))
        )
    ]
    for load in loads:
        load.start()
    loads[0].wait()
    loads[1].wait()
    sketch_parts = split(sketch[...])
    sketched = product(split(two[...].reshape(slices * local, width)), sketch_parts, NN)
    loads[2].wait()
    lanes = jnp.concatenate([sketched[n * local : (n + 1) * local] for n in range(slices)], axis=1)
    weights = jnp.concatenate([core[n] for n in range(slices)], axis=1)
    bridge_part[...] = product(split(lanes), split(weights), NT)
    loads[3].wait()
    pl.semaphore_wait(barrier, len(greeted))

    pending = []

    def swap(source, target, phase):
        copy = remote(source, target, swap_send.at[phase], swap_recv.at[phase], partner)
        copy.start()
        pending.append(copy)
        return copy

    def send_slices(source, target, phase):
        for peer in slice_peers:
            copy = remote(source, target, slice_send.at[phase, peer], slice_recv.at[phase, my_slice], slice_device(peer))
            copy.start()
            pending.append(copy)

    def land_slices(target_of, phase):
        for peer in slice_peers:
            place = target_of(peer)
            remote(place, place, slice_send.at[phase, peer], slice_recv.at[phase, peer], slice_device(peer)).wait_recv()

    def send_rank(source_of, target, phase):
        for peer in rank_peers:
            copy = remote(source_of(peer), target, rank_send.at[phase, peer], rank_recv.at[phase, my_rank], rank_device(peer))
            copy.start()
            pending.append(copy)

    def land_rank(target_of, phase):
        for peer in rank_peers:
            place = target_of(peer)
            remote(place, place, rank_send.at[phase, peer], rank_recv.at[phase, peer], rank_device(peer)).wait_recv()

    def total(ref, count):
        value = ref[0]
        for k in range(1, count):
            value = value + ref[k]
        return value

    own_rows = rows_of(my_rank, local)

    def send_two(first, last):
        for peer in rank_peers[first:last]:
            for slot in range(full):
                n = slot * n_rank + peer
                copy = remote(two.at[n], full_two.at[slot, own_rows, :], two_send.at[n], two_recv.at[slot, my_rank], rank_device(peer))
                copy.start()
                pending.append(copy)

    def extra_two(i, action):
        n, target_rank = full * n_rank + i, extra_owner(i)

        @pl.when(my_rank != target_rank)
        def _():
            copy = remote(two.at[n], full_two.at[full, own_rows, :], two_send.at[n], two_recv.at[full, my_rank], (my_cut, target_rank))
            action(copy)

    def keep_two():
        for slot in range(full):
            full_two[slot, own_rows, :] = two[slot * n_rank + my_rank]
        for i in range(extra):
            @pl.when(my_rank == extra_owner(i))
            def _():
                full_two[full, own_rows, :] = two[full * n_rank + i]

    def land_two(slot):
        for peer in rank_peers:
            place = full_two.at[slot, rows_of(peer, local), :]
            remote(place, place, two_send.at[0], two_recv.at[slot, peer], rank_device(peer)).wait_recv()

    def pieces(k):
        count = len(rank_peers)
        cuts = [0] + [round(count * part) for part in PIECES] + [count]
        send_two(cuts[k], cuts[k + 1])
        if k == EXTRA_PIECE:
            for i in range(extra):
                extra_two(i, lambda copy: copy.start())

    away_rows = pl.ds(pl.multiple_of((1 - my_core) * small, small), small)
    step = swap(bridge_part.at[away_rows, :], bridge_swap, 0)
    pieces(0)
    keep_two()
    step.wait_recv()
    bridge_slices[my_slice] = bridge_part[rows_of(my_core, small), :] + bridge_swap[...]
    send_slices(bridge_slices.at[my_slice], bridge_slices.at[my_slice], 0)
    one_high[...], one_low[...] = split(one[...].reshape(slices * local, width))
    one_parts = (one_high[...], one_low[...])
    square_high[...], square_low[...] = split(product(one_parts, one_parts, TN))
    land_slices(lambda peer: bridge_slices.at[peer], 0)
    own = bridge_half.at[my_core, rows_of(my_rank, small), :]
    own[...] = total(bridge_slices, n_slices)
    send_rank(lambda peer: own, own, 0)
    land_rank(lambda peer: bridge_half.at[my_core, rows_of(peer, small), :], 0)
    pieces(1)
    swap(bridge_half.at[my_core], bridge_half.at[my_core], 1).wait_recv()
    for r in range(n_rank):
        for h in range(2):
            bridge[r * local + h * small : r * local + (h + 1) * small, :] = bridge_half[h, r * small : (r + 1) * small, :]

    def put_part(index, rows_parts, matrix_parts, first=True):
        both = product(rows_parts, matrix_parts, TN)
        for h in range(2):
            piece = both[:, h * half_width : (h + 1) * half_width]
            part[index, h] = piece if first else part[index, h] + piece

    def reduce(index, between):
        step = swap(part.at[index, 1 - my_core], swapped.at[index], 2 + 2 * index)
        between[0]()
        step.wait_recv()
        half[index] = part[index, my_core] + swapped[index]
        recv_rank[index, my_rank] = half[index, rows_of(my_rank, band), :]
        send_rank(lambda peer: half.at[index, rows_of(peer, band), :], recv_rank.at[index, my_rank], 1 + 2 * index)
        between[1]()
        land_rank(lambda peer: recv_rank.at[index, peer], 1 + 2 * index)
        recv_slice[index, my_slice] = total(recv_rank.at[index], n_rank)
        place = recv_slice.at[index, my_slice]
        send_slices(place, place, 1 + index)
        between[2]()
        land_slices(lambda peer: recv_slice.at[index, peer], 1 + index)
        own = whole.at[index, my_core, rows_of(my_rank, band), :]
        own[...] = total(recv_slice.at[index], n_slices)
        earlier = list(pending)
        pending.clear()
        send_rank(lambda peer: own, own, 2 + 2 * index)
        between[3]()
        for copy in earlier:
            copy.wait_send()
        land_rank(lambda peer: whole.at[index, my_core, rows_of(peer, band), :], 2 + 2 * index)
        step = swap(whole.at[index, my_core], whole.at[index, my_core], 3 + 2 * index)
        step.wait_recv()
        return jnp.concatenate([whole[index, 0], whole[index, 1]], axis=1)

    def nothing():
        pass

    def rows_one():
        first_rows[...] = product((one_high[...], one_low[...]), split(bridge[...]), NN)

    put_part(0, split(bridge[...]), (square_high[...], square_low[...]))
    first_sum = split(reduce(0, (nothing, rows_one, lambda: pieces(2), lambda: pieces(3))))
    gram[...] = product(first_sum, split(bridge[...]), NN)
    inverse_factor(gram, gram_rows, gram_columns, out_width)
    first_carry = split(product(split(gram[...]), first_sum, NN))
    first_inverse = split(gram[...] * scale_left)

    for slot in range(slots):
        here = slice(slot * out_width, (slot + 1) * out_width)

        def project():
            land_two(slot)
            block = product(first_carry, split(full_two[slot]), NN)
            parts = split(block)
            rows = product(parts, sketch_parts, NN)
            second_rows[here, :] = rows
            put_part(1, split(rows), parts, slot == 0)

        if slot < full:
            project()
        else:
            pl.when(has_extra(my_rank))(project)

    def back(slot, peer):
        n = slot * n_rank + (my_rank if slot < full else extra_held(my_rank))
        source = second_rows.at[pl.ds(pl.multiple_of(slot * out_width + peer * band, 8), band), :]
        return remote(source, returned.at[n], back_send.at[slot, peer], back_recv.at[n], rank_device(peer))

    def give_back():
        for slot in range(slots):
            n = slot * n_rank + (my_rank if slot < full else extra_held(my_rank))

            def send_rows():
                returned[n] = second_rows[pl.ds(pl.multiple_of(slot * out_width + my_rank * band, 8), band), :]
                for peer in rank_peers:
                    back(slot, peer).start()
            if slot < full:
                send_rows()
            else:
                pl.when(has_extra(my_rank))(send_rows)

    def finish_left():
        ortho = product(split(first_rows[...]), first_inverse, NT)
        left[...] = ortho.reshape(slices, local, out_width)
        outs[0].start()

    def land_back():
        for n in range(slices):
            @pl.when(my_rank != (n % n_rank if n < full * n_rank else extra_owner(n - full * n_rank)))
            def _():
                remote(returned.at[n], returned.at[n], back_send.at[0, 0], back_recv.at[n], partner).wait_recv()
        outs[1].start()

    outs = [
        pltpu.make_async_copy(source, target, load_sem.at[k])
        for k, (source, target) in enumerate(((left, left_ref), (returned, returned_ref)))
    ]

    def land_and_finish():
        land_back()
        finish_left()
        for i in range(extra):
            extra_two(i, lambda copy: copy.wait_send())
        for slot in range(slots):
            def sent():
                for peer in rank_peers:
                    back(slot, peer).wait_send()
            if slot < full:
                sent()
            else:
                pl.when(has_extra(my_rank))(sent)

    second_sum = reduce(1, (nothing, nothing, give_back, land_and_finish))
    outs.append(pltpu.make_async_copy(whole.at[1], reduced_ref, load_sem.at[2]))
    outs[2].start()
    gram_ref[...] = product(split(second_sum), sketch_parts, NN)

    for copy in pending:
        copy.wait_send()
    for copy in outs:
        copy.wait()


def finish_kernel(
    scale_middle, gram_ref, reduced_ref, returned_ref, left_in_ref, left_ref, middle_ref, carry_ref,
    reduced, rows, held, gram, gram_rows, gram_columns, sems,
):
    loads = [
        pltpu.make_async_copy(source, target, sems.at[k])
        for k, (source, target) in enumerate(((left_in_ref, held), (returned_ref, rows), (reduced_ref, reduced)))
    ]
    for load in loads:
        load.start()
    slices, band, out_width = rows.shape
    gram[...] = gram_ref[...]
    inverse_factor(gram, gram_rows, gram_columns, out_width)
    loads[0].wait()
    out = pltpu.make_async_copy(held, left_ref, sems.at[3])
    out.start()
    inverse = split(gram[...])
    loads[2].wait()
    carry_ref[...] = product(inverse, split(jnp.concatenate([reduced[0], reduced[1]], axis=1)), NN)
    loads[1].wait()
    flat = rows[...].reshape(slices * band, out_width)
    middle = product(split(flat), split(gram[...] * scale_middle), NT)
    middle_ref[...] = middle.reshape(slices, band, out_width)
    out.wait()


def solution(mesh):
    n_cuts, n_rank = mesh.shape["cuts"], mesh.shape["rank"]

    def on_device(core_one, core_two, right_sketch, sketch_core):
        local, slices, width = core_one.shape
        out_width = right_sketch.shape[1]
        band, n_slices = out_width // n_rank, n_cuts // 2
        slots = -(-slices // n_rank)
        rows = local * slices
        scale_left = math.sqrt(local * n_rank * slices * n_cuts)
        scale_middle = math.sqrt(out_width * slices * n_cuts)
        vmem, sems = pltpu.VMEM, pltpu.SemaphoreType.DMA
        any_place, in_vmem = pl.BlockSpec(memory_space=pl.ANY), pl.BlockSpec(memory_space=pltpu.VMEM)
        left, returned, reduced, gram = pl.pallas_call(
            functools.partial(kernel, n_cuts, n_rank, scale_left),
            out_shape=(
                jax.ShapeDtypeStruct((slices, local, out_width), F32),
                jax.ShapeDtypeStruct((slices, band, out_width), F32),
                jax.ShapeDtypeStruct((2, out_width, width // 2), F32),
                jax.ShapeDtypeStruct((out_width, out_width), F32),
            ),
            in_specs=[any_place] * 4,
            out_specs=(any_place,) * 3 + (in_vmem,),
            scratch_shapes=[
                vmem((slices, local, width), F32),
                vmem((slices, local, width), F32),
                vmem((width, out_width), F32),
                vmem((slices, out_width, out_width), F32),
                vmem((rows, width), BF16),
                vmem((rows, width), BF16),
                vmem((width, width), BF16),
                vmem((width, width), BF16),
                vmem((local, out_width), F32),
                vmem((local // 2, out_width), F32),
                vmem((n_slices, local // 2, out_width), F32),
                vmem((2, width // 2, out_width), F32),
                vmem((width, out_width), F32),
                vmem((rows, out_width), F32),
                vmem((slots, width, width), F32),
                vmem((slots * out_width, out_width), F32),
                vmem((slices, band, out_width), F32),
                vmem((slices, local, out_width), F32),
                vmem((out_width, out_width), F32),
                vmem((16, out_width), F32),
                vmem((128, out_width), F32),
                vmem((2, 2, out_width, width // 2), F32),
                vmem((2, out_width, width // 2), F32),
                vmem((2, out_width, width // 2), F32),
                vmem((2, n_rank, band, width // 2), F32),
                vmem((2, n_slices, band, width // 2), F32),
                vmem((2, 2, out_width, width // 2), F32),
                sems((4,)),
                sems((6,)),
                sems((6,)),
                sems((3, n_slices)),
                sems((3, n_slices)),
                sems((5, n_rank)),
                sems((5, n_rank)),
                sems((slices,)),
                sems((slots, n_rank)),
                sems((slots, n_rank)),
                sems((slices,)),
            ],
            compiler_params=pltpu.CompilerParams(
                collective_id=0, has_side_effects=True, vmem_limit_bytes=60 * 1024 * 1024
            ),
        )(
            core_one.transpose(1, 0, 2), core_two.transpose(1, 0, 2),
            right_sketch, sketch_core.transpose(1, 0, 2),
        )
        left, middle, carry = pl.pallas_call(
            functools.partial(finish_kernel, scale_middle),
            out_shape=(
                jax.ShapeDtypeStruct((slices, local, out_width), F32),
                jax.ShapeDtypeStruct((slices, band, out_width), F32),
                jax.ShapeDtypeStruct((out_width, width), F32),
            ),
            in_specs=[in_vmem] + [any_place] * 3,
            out_specs=(any_place, in_vmem, in_vmem),
            scratch_shapes=[
                vmem((2, out_width, width // 2), F32),
                vmem((slices, band, out_width), F32),
                vmem((slices, local, out_width), F32),
                vmem((out_width, out_width), F32),
                vmem((16, out_width), F32),
                vmem((128, out_width), F32),
                sems((4,)),
            ],
        )(gram, reduced, returned, left)
        return left.transpose(1, 0, 2), middle.transpose(1, 0, 2), carry

    placed = (P("rank", "cuts", None), P("rank", "cuts", None), P(), P(None, "cuts", None))
    return jax.shard_map(
        on_device,
        mesh=mesh,
        in_specs=placed,
        out_specs=(P("rank", "cuts", None), P("rank", "cuts", None), P()),
        check_vma=False,
    )
```

```python
import functools
import math

import jax
import jax.numpy as jnp
from jax import lax
from jax.experimental import pallas as pl
from jax.experimental.pallas import tpu as pltpu
from jax.sharding import PartitionSpec as P

MESH = pl.DeviceIdType.MESH
F32 = jnp.float32
BF16 = jnp.bfloat16
NN = (((1,), (0,)), ((), ()))
NT = (((1,), (1,)), ((), ()))
TN = (((0,), (0,)), ((), ()))
PIECES = (0.4, 0.4, 0.6667)
EXTRA_PIECE = 1


def split(value):
    high = value.astype(BF16)
    return high, (value - high.astype(F32)).astype(BF16)


def product(left, right, dims):
    (left_high, left_low), (right_high, right_low) = left, right
    dot = functools.partial(lax.dot_general, dimension_numbers=dims, preferred_element_type=F32)
    return dot(left_high, right_high) + (dot(left_high, right_low) + dot(left_low, right_high))


def inverse_factor(gram_ref, rows_ref, columns_ref, width):
    blocks = width // 8
    lane = lax.broadcasted_iota(jnp.int32, (8, width), 1)
    row = lax.broadcasted_iota(jnp.int32, (8, width), 0)
    rest = gram_ref[...].reshape(blocks, 8, width)
    own, rest = rest[0], rest[1:]
    for block in range(blocks):
        base = 8 * block
        last = block + 1 == blocks
        inside = jnp.logical_and(lane >= base, lane < base + 8)
        slot = (block % 2) * 8
        for m in range(8):
            columns_ref[(slot + m) * 8 : (slot + m + 1) * 8, :] = jnp.broadcast_to(own[:, base + m : base + m + 1], (8, width))
        rows_ref[slot : slot + 8, :] = jnp.where(inside, (lane == row + base).astype(F32), own)
        entry = [
            [jnp.broadcast_to(columns_ref[(slot + m) * 8 + i : (slot + m) * 8 + i + 1, :], (8, width)) if m <= i else None for m in range(8)]
            for i in range(8)
        ]
        rows = [jnp.broadcast_to(rows_ref[slot + i : slot + i + 1, :], (8, width)) for i in range(8)]
        if not last:
            ahead = [jnp.broadcast_to(rest[0][:, base + m : base + m + 1], (8, width)) for m in range(8)]
            following = jnp.where(inside, 0.0, rest[0])
        inverse, solved = [], []
        for j in range(8):
            inverse.append(lax.rsqrt(entry[j][j]))
            solved.append(rows[j] * inverse[j])
            for i in range(j + 1, 8):
                entry[i][j] = entry[i][j] * inverse[j]
            for i in range(j + 1, 8):
                rows[i] = rows[i] - entry[i][j] * solved[j]
                for m in range(j + 1, i + 1):
                    entry[i][m] = entry[i][m] - entry[i][j] * entry[m][j]
            if not last:
                factor = ahead[j] * inverse[j]
                following = following - factor * solved[j]
                for m in range(j + 1, 8):
                    ahead[m] = ahead[m] - factor * entry[m][j]
        done = solved[0]
        for j in range(1, 8):
            done = jnp.where(row == j, solved[j], done)
        gram_ref[base : base + 8, :] = jnp.where(lane <= row + base, done, 0.0)
        if last:
            break
        own, rest = following, rest[1:]
        if block + 2 == blocks:
            continue
        back = list(solved)
        for j in reversed(range(8)):
            for i in range(j + 1, 8):
                back[j] = back[j] - entry[i][j] * back[i]
            back[j] = back[j] * inverse[j]
        update = jnp.where(inside[None], 0.0, rest)
        for m in range(8):
            update = update - rest[:, :, base + m : base + m + 1] * back[m][None]
        rest = update


def kernel(
    n_cuts, n_rank, scale_left,
    one_ref, two_ref, sketch_ref, core_ref, left_ref, returned_ref, reduced_ref, gram_ref,
    one, two, sketch, core, one_high, one_low, square_high, square_low,
    bridge_part, bridge_swap, bridge_slices, bridge_half, bridge,
    first_rows, full_two, second_rows, returned, left, gram, gram_rows, gram_columns,
    part, swapped, half, recv_rank, recv_slice, whole,
    load_sem, swap_send, swap_recv, slice_send, slice_recv, rank_send, rank_recv,
    two_send, two_recv, back_send, back_recv,
):
    slices, local, width = one_ref.shape
    out_width = sketch_ref.shape[1]
    band = out_width // n_rank
    small, half_width = local // 2, width // 2
    n_slices = n_cuts // 2
    side = math.isqrt(n_rank)
    side = side if side * side == n_rank else n_rank
    other = n_rank // side
    my_cut, my_rank = lax.axis_index("cuts"), lax.axis_index("rank")
    my_slice, my_core = lax.div(my_cut, 2), lax.rem(my_cut, 2)
    full, extra = slices // n_rank, slices % n_rank
    stride = max((n_rank - 1) // (extra - 1), 1) if extra > 1 else 1
    slots = full + (1 if extra else 0)

    square = extra == side and side == other

    def extra_owner(i):
        return i * other + lax.rem(i + 2 * my_core, other) if square else i * stride

    def extra_held(rank):
        return lax.div(rank, other if square else stride)

    def has_extra(rank):
        held = extra_held(rank)
        return jnp.logical_and(held < extra, rank == extra_owner(held))

    def away(step, length):
        return min(step, length - step)

    partner = (my_cut + 1 - 2 * my_core, my_rank)
    slice_steps = sorted(range(1, n_slices), key=lambda k: -away(k, n_slices))
    slice_peers = [lax.rem(my_slice + k, n_slices) for k in slice_steps]
    rank_steps = sorted(
        ((i, j) for i in range(side) for j in range(other) if i or j),
        key=lambda t: -(away(t[0], side) + away(t[1], other)),
    )
    rank_peers = [
        lax.rem(lax.div(my_rank, other) + i, side) * other + lax.rem(lax.rem(my_rank, other) + j, other)
        for i, j in rank_steps
    ]

    def slice_device(peer):
        return (peer * 2 + my_core, my_rank)

    def rank_device(peer):
        return (my_cut, peer)

    def remote(source, target, send, recv, device):
        return pltpu.make_async_remote_copy(
            src_ref=source, dst_ref=target, send_sem=send, recv_sem=recv,
            device_id=device, device_id_type=MESH,
        )

    def rows_of(index, size):
        return pl.ds(pl.multiple_of(index * size, size), size)

    barrier = pltpu.get_barrier_semaphore()
    greeted = [partner] + [slice_device(p) for p in slice_peers] + [rank_device(p) for p in rank_peers]
    for device in greeted:
        pl.semaphore_signal(barrier, inc=1, device_id=device, device_id_type=MESH)
    loads = [
        pltpu.make_async_copy(source, target, load_sem.at[k])
        for k, (source, target) in enumerate(
            ((two_ref, two), (sketch_ref, sketch), (core_ref, core), (one_ref, one))
        )
    ]
    for load in loads:
        load.start()
    loads[0].wait()
    loads[1].wait()
    sketch_parts = split(sketch[...])
    sketched = product(split(two[...].reshape(slices * local, width)), sketch_parts, NN)
    loads[2].wait()
    lanes = jnp.concatenate([sketched[n * local : (n + 1) * local] for n in range(slices)], axis=1)
    weights = jnp.concatenate([core[n] for n in range(slices)], axis=1)
    bridge_part[...] = product(split(lanes), split(weights), NT)
    loads[3].wait()
    pl.semaphore_wait(barrier, len(greeted))

    pending = []

    def swap(source, target, phase):
        copy = remote(source, target, swap_send.at[phase], swap_recv.at[phase], partner)
        copy.start()
        pending.append(copy)
        return copy

    def send_slices(source, target, phase):
        for peer in slice_peers:
            copy = remote(source, target, slice_send.at[phase, peer], slice_recv.at[phase, my_slice], slice_device(peer))
            copy.start()
            pending.append(copy)

    def land_slices(target_of, phase):
        for peer in slice_peers:
            place = target_of(peer)
            remote(place, place, slice_send.at[phase, peer], slice_recv.at[phase, peer], slice_device(peer)).wait_recv()

    def send_rank(source_of, target, phase):
        for peer in rank_peers:
            copy = remote(source_of(peer), target, rank_send.at[phase, peer], rank_recv.at[phase, my_rank], rank_device(peer))
            copy.start()
            pending.append(copy)

    def land_rank(target_of, phase):
        for peer in rank_peers:
            place = target_of(peer)
            remote(place, place, rank_send.at[phase, peer], rank_recv.at[phase, peer], rank_device(peer)).wait_recv()

    def total(ref, count):
        value = ref[0]
        for k in range(1, count):
            value = value + ref[k]
        return value

    own_rows = rows_of(my_rank, local)

    def send_two(first, last):
        for peer in rank_peers[first:last]:
            for slot in range(full):
                n = slot * n_rank + peer
                copy = remote(two.at[n], full_two.at[slot, own_rows, :], two_send.at[n], two_recv.at[slot, my_rank], rank_device(peer))
                copy.start()
                pending.append(copy)

    def extra_two(i, action):
        n, target_rank = full * n_rank + i, extra_owner(i)

        @pl.when(my_rank != target_rank)
        def _():
            copy = remote(two.at[n], full_two.at[full, own_rows, :], two_send.at[n], two_recv.at[full, my_rank], (my_cut, target_rank))
            action(copy)

    def keep_two():
        for slot in range(full):
            full_two[slot, own_rows, :] = two[slot * n_rank + my_rank]
        for i in range(extra):
            @pl.when(my_rank == extra_owner(i))
            def _():
                full_two[full, own_rows, :] = two[full * n_rank + i]

    def land_two(slot):
        for peer in rank_peers:
            place = full_two.at[slot, rows_of(peer, local), :]
            remote(place, place, two_send.at[0], two_recv.at[slot, peer], rank_device(peer)).wait_recv()

    def pieces(k):
        count = len(rank_peers)
        cuts = [0] + [round(count * part) for part in PIECES] + [count]
        send_two(cuts[k], cuts[k + 1])
        if k == EXTRA_PIECE:
            for i in range(extra):
                extra_two(i, lambda copy: copy.start())

    away_rows = pl.ds(pl.multiple_of((1 - my_core) * small, small), small)
    step = swap(bridge_part.at[away_rows, :], bridge_swap, 0)
    pieces(0)
    keep_two()
    step.wait_recv()
    bridge_slices[my_slice] = bridge_part[rows_of(my_core, small), :] + bridge_swap[...]
    send_slices(bridge_slices.at[my_slice], bridge_slices.at[my_slice], 0)
    one_high[...], one_low[...] = split(one[...].reshape(slices * local, width))
    one_parts = (one_high[...], one_low[...])
    square_high[...], square_low[...] = split(product(one_parts, one_parts, TN))
    land_slices(lambda peer: bridge_slices.at[peer], 0)
    own = bridge_half.at[my_core, rows_of(my_rank, small), :]
    own[...] = total(bridge_slices, n_slices)
    send_rank(lambda peer: own, own, 0)
    land_rank(lambda peer: bridge_half.at[my_core, rows_of(peer, small), :], 0)
    pieces(1)
    swap(bridge_half.at[my_core], bridge_half.at[my_core], 1).wait_recv()
    for r in range(n_rank):
        for h in range(2):
            bridge[r * local + h * small : r * local + (h + 1) * small, :] = bridge_half[h, r * small : (r + 1) * small, :]

    def put_part(index, rows_parts, matrix_parts, first=True):
        both = product(rows_parts, matrix_parts, TN)
        for h in range(2):
            piece = both[:, h * half_width : (h + 1) * half_width]
            part[index, h] = piece if first else part[index, h] + piece

    def reduce(index, right_ref, between):
        def half_gram(core):
            return product(split(whole[index, core]), split(right_ref[rows_of(core, half_width), :]), NN)

        step = swap(part.at[index, 1 - my_core], swapped.at[index], 2 + 2 * index)
        between[0]()
        step.wait_recv()
        half[index] = part[index, my_core] + swapped[index]
        recv_rank[index, my_rank] = half[index, rows_of(my_rank, band), :]
        send_rank(lambda peer: half.at[index, rows_of(peer, band), :], recv_rank.at[index, my_rank], 1 + 2 * index)
        between[1]()
        land_rank(lambda peer: recv_rank.at[index, peer], 1 + 2 * index)
        recv_slice[index, my_slice] = total(recv_rank.at[index], n_rank)
        place = recv_slice.at[index, my_slice]
        send_slices(place, place, 1 + index)
        between[2]()
        land_slices(lambda peer: recv_slice.at[index, peer], 1 + index)
        own = whole.at[index, my_core, rows_of(my_rank, band), :]
        own[...] = total(recv_slice.at[index], n_slices)
        earlier = list(pending)
        pending.clear()
        send_rank(lambda peer: own, own, 2 + 2 * index)
        between[3]()
        for copy in earlier:
            copy.wait_send()
        land_rank(lambda peer: whole.at[index, my_core, rows_of(peer, band), :], 2 + 2 * index)
        step = swap(whole.at[index, my_core], whole.at[index, my_core], 3 + 2 * index)
        own_gram = half_gram(my_core)
        step.wait_recv()
        return own_gram + half_gram(1 - my_core), jnp.concatenate([whole[index, 0], whole[index, 1]], axis=1)

    def nothing():
        pass

    def rows_one():
        first_rows[...] = product((one_high[...], one_low[...]), split(bridge[...]), NN)

    put_part(0, split(bridge[...]), (square_high[...], square_low[...]))
    gram[...], first_sum = reduce(0, bridge, (nothing, rows_one, lambda: pieces(2), lambda: pieces(3)))
    first_sum = split(first_sum)
    inverse_factor(gram, gram_rows, gram_columns, out_width)
    first_carry = split(product(split(gram[...]), first_sum, NN))
    first_inverse = split(gram[...] * scale_left)

    for slot in range(slots):
        here = slice(slot * out_width, (slot + 1) * out_width)

        def project():
            land_two(slot)
            block = product(first_carry, split(full_two[slot]), NN)
            parts = split(block)
            rows = product(parts, sketch_parts, NN)
            second_rows[here, :] = rows
            put_part(1, split(rows), parts, slot == 0)

        if slot < full:
            project()
        else:
            pl.when(has_extra(my_rank))(project)

    def back(slot, peer):
        n = slot * n_rank + (my_rank if slot < full else extra_held(my_rank))
        source = second_rows.at[pl.ds(pl.multiple_of(slot * out_width + peer * band, 8), band), :]
        return remote(source, returned.at[n], back_send.at[slot, peer], back_recv.at[n], rank_device(peer))

    def give_back():
        for slot in range(slots):
            n = slot * n_rank + (my_rank if slot < full else extra_held(my_rank))

            def send_rows():
                returned[n] = second_rows[pl.ds(pl.multiple_of(slot * out_width + my_rank * band, 8), band), :]
                for peer in rank_peers:
                    back(slot, peer).start()
            if slot < full:
                send_rows()
            else:
                pl.when(has_extra(my_rank))(send_rows)

    def finish_left():
        ortho = product(split(first_rows[...]), first_inverse, NT)
        left[...] = ortho.reshape(slices, local, out_width)
        outs[0].start()

    def land_back():
        for n in range(slices):
            @pl.when(my_rank != (n % n_rank if n < full * n_rank else extra_owner(n - full * n_rank)))
            def _():
                remote(returned.at[n], returned.at[n], back_send.at[0, 0], back_recv.at[n], partner).wait_recv()
        outs[1].start()

    outs = [
        pltpu.make_async_copy(source, target, load_sem.at[k])
        for k, (source, target) in enumerate(((left, left_ref), (returned, returned_ref)))
    ]

    def land_and_finish():
        land_back()
        finish_left()
        for i in range(extra):
            extra_two(i, lambda copy: copy.wait_send())
        for slot in range(slots):
            def sent():
                for peer in rank_peers:
                    back(slot, peer).wait_send()
            if slot < full:
                sent()
            else:
                pl.when(has_extra(my_rank))(sent)

    gram_ref[...], _ = reduce(1, sketch, (nothing, nothing, give_back, land_and_finish))
    outs.append(pltpu.make_async_copy(whole.at[1], reduced_ref, load_sem.at[2]))
    outs[2].start()

    for copy in pending:
        copy.wait_send()
    for copy in outs:
        copy.wait()


def finish_kernel(
    scale_middle, gram_ref, reduced_ref, returned_ref, left_in_ref, left_ref, middle_ref, carry_ref,
    reduced, rows, held, gram, gram_rows, gram_columns, sems,
):
    loads = [
        pltpu.make_async_copy(source, target, sems.at[k])
        for k, (source, target) in enumerate(((left_in_ref, held), (returned_ref, rows), (reduced_ref, reduced)))
    ]
    for load in loads:
        load.start()
    slices, band, out_width = rows.shape
    gram[...] = gram_ref[...]
    inverse_factor(gram, gram_rows, gram_columns, out_width)
    loads[0].wait()
    out = pltpu.make_async_copy(held, left_ref, sems.at[3])
    out.start()
    inverse = split(gram[...])
    loads[2].wait()
    carry_ref[...] = product(inverse, split(jnp.concatenate([reduced[0], reduced[1]], axis=1)), NN)
    loads[1].wait()
    flat = rows[...].reshape(slices * band, out_width)
    middle = product(split(flat), split(gram[...] * scale_middle), NT)
    middle_ref[...] = middle.reshape(slices, band, out_width)
    out.wait()


def solution(mesh):
    n_cuts, n_rank = mesh.shape["cuts"], mesh.shape["rank"]

    def on_device(core_one, core_two, right_sketch, sketch_core):
        local, slices, width = core_one.shape
        out_width = right_sketch.shape[1]
        band, n_slices = out_width // n_rank, n_cuts // 2
        slots = -(-slices // n_rank)
        rows = local * slices
        scale_left = math.sqrt(local * n_rank * slices * n_cuts)
        scale_middle = math.sqrt(out_width * slices * n_cuts)
        vmem, sems = pltpu.VMEM, pltpu.SemaphoreType.DMA
        any_place, in_vmem = pl.BlockSpec(memory_space=pl.ANY), pl.BlockSpec(memory_space=pltpu.VMEM)
        left, returned, reduced, gram = pl.pallas_call(
            functools.partial(kernel, n_cuts, n_rank, scale_left),
            out_shape=(
                jax.ShapeDtypeStruct((slices, local, out_width), F32),
                jax.ShapeDtypeStruct((slices, band, out_width), F32),
                jax.ShapeDtypeStruct((2, out_width, width // 2), F32),
                jax.ShapeDtypeStruct((out_width, out_width), F32),
            ),
            in_specs=[any_place] * 4,
            out_specs=(any_place,) * 3 + (in_vmem,),
            scratch_shapes=[
                vmem((slices, local, width), F32),
                vmem((slices, local, width), F32),
                vmem((width, out_width), F32),
                vmem((slices, out_width, out_width), F32),
                vmem((rows, width), BF16),
                vmem((rows, width), BF16),
                vmem((width, width), BF16),
                vmem((width, width), BF16),
                vmem((local, out_width), F32),
                vmem((local // 2, out_width), F32),
                vmem((n_slices, local // 2, out_width), F32),
                vmem((2, width // 2, out_width), F32),
                vmem((width, out_width), F32),
                vmem((rows, out_width), F32),
                vmem((slots, width, width), F32),
                vmem((slots * out_width, out_width), F32),
                vmem((slices, band, out_width), F32),
                vmem((slices, local, out_width), F32),
                vmem((out_width, out_width), F32),
                vmem((16, out_width), F32),
                vmem((128, out_width), F32),
                vmem((2, 2, out_width, width // 2), F32),
                vmem((2, out_width, width // 2), F32),
                vmem((2, out_width, width // 2), F32),
                vmem((2, n_rank, band, width // 2), F32),
                vmem((2, n_slices, band, width // 2), F32),
                vmem((2, 2, out_width, width // 2), F32),
                sems((4,)),
                sems((6,)),
                sems((6,)),
                sems((3, n_slices)),
                sems((3, n_slices)),
                sems((5, n_rank)),
                sems((5, n_rank)),
                sems((slices,)),
                sems((slots, n_rank)),
                sems((slots, n_rank)),
                sems((slices,)),
            ],
            compiler_params=pltpu.CompilerParams(
                collective_id=0, has_side_effects=True, vmem_limit_bytes=60 * 1024 * 1024
            ),
        )(
            core_one.transpose(1, 0, 2), core_two.transpose(1, 0, 2),
            right_sketch, sketch_core.transpose(1, 0, 2),
        )
        left, middle, carry = pl.pallas_call(
            functools.partial(finish_kernel, scale_middle),
            out_shape=(
                jax.ShapeDtypeStruct((slices, local, out_width), F32),
                jax.ShapeDtypeStruct((slices, band, out_width), F32),
                jax.ShapeDtypeStruct((out_width, width), F32),
            ),
            in_specs=[in_vmem] + [any_place] * 3,
            out_specs=(any_place, in_vmem, in_vmem),
            scratch_shapes=[
                vmem((2, out_width, width // 2), F32),
                vmem((slices, band, out_width), F32),
                vmem((slices, local, out_width), F32),
                vmem((out_width, out_width), F32),
                vmem((16, out_width), F32),
                vmem((128, out_width), F32),
                sems((4,)),
            ],
        )(gram, reduced, returned, left)
        return left.transpose(1, 0, 2), middle.transpose(1, 0, 2), carry

    placed = (P("rank", "cuts", None), P("rank", "cuts", None), P(), P(None, "cuts", None))
    return jax.shard_map(
        on_device,
        mesh=mesh,
        in_specs=placed,
        out_specs=(P("rank", "cuts", None), P("rank", "cuts", None), P()),
        check_vma=False,
    )
```
